512 devices in a mesh: dp: 16 (over z, core), expert: 32 (over y, x).
Axes of the slice: x: 4, y: 8, z: 8, core: 2. Of those that a mesh axis runs over, the one named last changes fastest.
Arguments:
- tokens: bfloat16 [65536, 2048], P(('dp', 'expert')), may hold values from -6 to 6
- gates: float32 [65536, 2], P(('dp', 'expert')), may hold values from 0.1 to 1
- experts: int32 [65536, 2], P(('dp', 'expert')), may hold values from 0 to 31, all different within a row; in each aligned block of 128 rows (0 to 127, 128 to 255, ...) at most 12 rows name the same one
- gate_weight: bfloat16 [32, 2048, 512], P('expert', 'dp'), may hold values from -0.125 to 0.125
- up_weight: bfloat16 [32, 2048, 512], P('expert', 'dp'), may hold values from -0.125 to 0.125
- down_weight: bfloat16 [32, 2048, 512], P('expert', 'dp'), may hold values from -0.25 to 0.25
- out_grad: bfloat16 [65536, 2048], P(('dp', 'expert')), may hold values from -6 to 6
Outputs:
- mixed: bfloat16 [65536, 2048], P(('dp', 'expert'))
- token_grad: bfloat16 [65536, 2048], P(('dp', 'expert'))
- gate_grad: float32 [65536, 2], P(('dp', 'expert'))
- gate_weight_grad: float32 [32, 2048, 512], P('expert', 'dp')
- up_weight_grad: float32 [32, 2048, 512], P('expert', 'dp')
The draws below stay inside these ranges and needn't reach their ends.
Inputs may be any that keep to these rules, and one draw needn't show every extreme that they name: The two experts of a token differ. Among the tokens of one device (aligned blocks of 128 rows) no expert is named by more than 12 picks, a bound that some block reaches.
All inputs are finite; a program needn't handle non-finite values.
Results may differ from the reference program's by a relative error of at most 0.02.
Values may be sent and summed in bfloat16 or wider, within the bound.
No kernel may reach another device: no remote copies, remote signals or barrier semaphores. Data moves between devices by JAX's collectives and lax.ppermute only.
A program may use at most 64 MiB of HBM per device.

```python
import math
import jax
import jax.numpy as jnp
import numpy as np
from jax import lax

D = 2048
H = 512
TOK_DEV = 128
EXPERTS = 32
CAP = 12
TOKENS = 65536
N_DP = 16
N_EXPERT = 32


def level_of(stream_key, shape, shards, low, top_value):
    loudness = 1.0
    for position, blocks in shards:
        steps = jax.random.uniform(jax.random.fold_in(jax.random.fold_in(stream_key, 6), position), (blocks,), jnp.float32, low / len(shards), top_value / len(shards))
        loudness = loudness * jnp.repeat(jnp.exp(steps), shape[position] // blocks).reshape((-1,) + (1,) * (len(shape) - 1 - position))
    return loudness


def deal_out(key, own, number, rows, count, top, most, lean):
    sequence = jax.random.permutation(key, count)
    heavy_load, common = load_shares(count, rows * top, most, lean, True), load_shares(count, rows * top, most, lean, False)
    places = jnp.arange(count)

    def named(sizes, offset_by):
        used = int((sizes > 0).sum())
        fixed = max(1, used // 4)
        shifted = fixed + (places - fixed + offset_by * (used - fixed)) % max(1, count - fixed)
        return jnp.zeros((count,), jnp.int32).at[sequence[jnp.where(places < fixed, places, shifted)]].set(jnp.asarray(sizes, jnp.int32))

    sizes = jnp.where(number % 4 == 0, named(heavy_load, number // 4), named(common, number - number // 4 - 1))
    mixed = jax.random.permutation(jax.random.fold_in(own, 3), count)
    donor, receiver = mixed[0:count // 2 * 2:2], mixed[1:count // 2 * 2:2]
    margin = jnp.minimum(sizes[donor] - 1, most - sizes[receiver]) // 2
    margin = jnp.where((donor == sequence[0]) | (receiver == sequence[0]) | (sizes[receiver] == 0), 0, jnp.maximum(margin, 0))
    shifted = jax.random.randint(jax.random.fold_in(own, 4), (count // 2,), 0, 1 << 20) % (margin + 1)
    sizes = sizes.at[donor].add(-shifted).at[receiver].add(shifted)
    items = jnp.searchsorted(jnp.cumsum(sizes), jnp.arange(rows * top), side="right").astype(jnp.int32)
    listing = items.reshape(top, rows).T
    listing = listing[jax.random.permutation(jax.random.fold_in(own, 1), rows)]
    offset_by = jax.random.randint(jax.random.fold_in(own, 2), (rows, 1), 0, top)
    return jnp.take_along_axis(listing, (jnp.arange(top)[None, :] + offset_by) % top, axis=1)


def load_shares(count, total, bound, slope, full):
    weights = [(1 << 20) // math.isqrt(rank ** slope) + 1 for rank in range(1, count + 1)]
    largest = bound if full else min(bound, max(-(-total // count), total * weights[0] // sum(weights)))
    least = 1 if total - largest >= count - 1 else 0
    holding, rest = [largest] + [least] * (count - 1), total - largest - least * (count - 1)
    while rest > 0:
        free = [i for i in range(1, count) if holding[i] < largest] or [i for i in range(1, count) if holding[i] < bound]
        whole, budget = sum([weights[i] for i in free]), rest
        for i in free:
            extra = min(bound - holding[i], max(1, budget * weights[i] // whole), rest)
            holding[i] = holding[i] + extra
            rest = rest - extra
    return np.array(holding)


def bell_draw(own_key, shape, deviation, most, shards=(), kind=jnp.bfloat16):
    result = deviation * jax.random.normal(own_key, shape, jnp.float32)
    if shards:
        result = result * level_of(own_key, shape, shards, -0.22, 0.18)
    return jnp.clip(result, -most, most).astype(kind)


def setup_inputs(seed: int = 0) -> dict:
    key_of = jax.random.split(jax.random.key(seed), 8)
    tokens = bell_draw(key_of[0], (TOKENS, D), 1.0, 6.0, ((0, 512),))
    gates = jnp.clip(0.1 + 0.9 * jax.random.uniform(key_of[1], (TOKENS, 2), jnp.float32) ** level_of(key_of[1], (TOKENS, 2), ((0, 512),), -0.2, 0.2), 0.1, 1.0)
    experts_keys = jax.random.split(jax.random.fold_in(key_of[2], 1), TOKENS // TOK_DEV)
    experts_turns = jax.random.permutation(jax.random.fold_in(key_of[2], 3), TOKENS // TOK_DEV)
    experts = jax.vmap(lambda own, number: deal_out(jax.random.fold_in(key_of[2], 2), own, number, TOK_DEV, EXPERTS, 2, CAP, 2))(experts_keys, experts_turns).reshape((TOKENS, 2))
    gate_weight = bell_draw(key_of[3], (EXPERTS, D, H), D ** -0.5, 0.125, ((0, 32), (1, 16)))
    up_weight = bell_draw(key_of[4], (EXPERTS, D, H), D ** -0.5, 0.125, ((0, 32), (1, 16)))
    down_weight = bell_draw(key_of[5], (EXPERTS, D, H), H ** -0.5, 0.25, ((0, 32), (1, 16)))
    out_grad = bell_draw(key_of[6], (TOKENS, D), 1.0, 6.0, ((0, 512),))
    return {"tokens": tokens, "gates": gates, "experts": experts, "gate_weight": gate_weight, "up_weight": up_weight, "down_weight": down_weight, "out_grad": out_grad}


def slot_tables(block_ids, experts_all, capacity):
    picked_ids = block_ids.reshape(-1)
    pick_count = picked_ids.shape[0]
    onehot = (picked_ids[:, None] == jnp.arange(experts_all, dtype=jnp.int32)[None, :]).astype(jnp.int32)
    before = jnp.cumsum(onehot, axis=0) - onehot
    slot_index = jnp.sum(before * onehot, axis=1).astype(jnp.int32)
    flat_slot = (picked_ids * capacity + slot_index).astype(jnp.int32)
    slot_owner = jnp.full((experts_all * capacity,), pick_count, jnp.int32)
    slot_owner = slot_owner.at[flat_slot].set(jnp.arange(pick_count, dtype=jnp.int32))
    return slot_owner, flat_slot


def group_partial(left, right):
    partial_sum = jnp.einsum('grd,grh->gdh', left.astype(jnp.float32), right.astype(jnp.float32))
    rounded = lax.optimization_barrier(partial_sum.astype(jnp.bfloat16))
    return jnp.sum(rounded.astype(jnp.float32), axis=0)


def reference(tokens, gates, experts, gate_weight, up_weight, down_weight, out_grad):
    blocks = N_DP * N_EXPERT
    picks_dev = 2 * TOK_DEV
    owners, flats = jax.vmap(lambda block_ids: slot_tables(block_ids, EXPERTS, CAP))(experts.reshape(blocks, TOK_DEV, 2))
    offsets = jnp.arange(blocks, dtype=jnp.int32)[:, None] * picks_dev
    global_pick = jnp.where(owners < picks_dev, owners + offsets, 2 * TOKENS).astype(jnp.int32)
    global_pick = global_pick.reshape(blocks, EXPERTS, CAP).transpose(1, 0, 2)
    tok_pad = jnp.concatenate([tokens, jnp.zeros((1, D), tokens.dtype)], axis=0)
    grad_pad = jnp.concatenate([out_grad, jnp.zeros((1, D), out_grad.dtype)], axis=0)
    gate_pad = jnp.concatenate([gates.reshape(-1), jnp.zeros((1,), jnp.float32)], axis=0)

    def per_expert(carry, inputs):
        mixed_acc, dx_acc, dg_acc = carry
        pick_rows, w_gate, w_up, w_down = inputs
        pick_flat = pick_rows.reshape(-1)
        tok_index = jnp.where(pick_flat < 2 * TOKENS, pick_flat // 2, TOKENS).astype(jnp.int32)
        rows_in = tok_pad[tok_index]
        rows_dy = grad_pad[tok_index]
        slot_gate = gate_pad[pick_flat]
        gate_pre = jnp.dot(rows_in, w_gate, preferred_element_type=jnp.float32)
        up_pre = jnp.dot(rows_in, w_up, preferred_element_type=jnp.float32)
        sigma_gate = jax.nn.sigmoid(gate_pre)
        hidden = (gate_pre * sigma_gate * up_pre).astype(jnp.bfloat16)
        expert_out = lax.dot_general(hidden, w_down, (((1,), (1,)), ((), ())), preferred_element_type=jnp.float32).astype(jnp.bfloat16)
        out_f = expert_out.astype(jnp.float32)
        mixed_acc = mixed_acc.at[tok_index].add(slot_gate[:, None] * out_f)
        dg_acc = dg_acc.at[pick_flat].add(jnp.sum(rows_dy.astype(jnp.float32) * out_f, axis=1))
        slot_grad = (slot_gate[:, None] * rows_dy.astype(jnp.float32)).astype(jnp.bfloat16)
        hidden_grad = jnp.dot(slot_grad, w_down, preferred_element_type=jnp.float32)
        up_grad = (hidden_grad * gate_pre * sigma_gate).astype(jnp.bfloat16)
        pre_grad = (hidden_grad * up_pre * sigma_gate * (1.0 + gate_pre * (1.0 - sigma_gate))).astype(jnp.bfloat16)
        row_grad = lax.dot_general(pre_grad, w_gate, (((1,), (1,)), ((), ())), preferred_element_type=jnp.float32)
        row_grad = row_grad + lax.dot_general(up_grad, w_up, (((1,), (1,)), ((), ())), preferred_element_type=jnp.float32)
        row_grad = row_grad.astype(jnp.bfloat16)
        dx_acc = dx_acc.at[tok_index].add(row_grad.astype(jnp.float32))
        grouped_in = rows_in.reshape(N_DP, -1, D)
        grad_g = group_partial(grouped_in, pre_grad.reshape(N_DP, -1, H))
        grad_u = group_partial(grouped_in, up_grad.reshape(N_DP, -1, H))
        return (mixed_acc, dx_acc, dg_acc), (grad_g, grad_u)

    start = (jnp.zeros((TOKENS + 1, D), jnp.float32), jnp.zeros((TOKENS + 1, D), jnp.float32), jnp.zeros((2 * TOKENS + 1,), jnp.float32))
    finals, grads = lax.scan(per_expert, start, (global_pick, gate_weight, up_weight, down_weight))
    mixed_acc, dx_acc, dg_acc = finals
    mixed = mixed_acc[:TOKENS].astype(jnp.bfloat16)
    token_grad = dx_acc[:TOKENS].astype(jnp.bfloat16)
    gate_grad = dg_acc[:2 * TOKENS].reshape(TOKENS, 2)
    return (mixed, token_grad, gate_grad, grads[0], grads[1])
```

```python
import jax
import jax.numpy as jnp
from jax import lax
from jax.experimental import pallas as pl
from jax.experimental.pallas import tpu as pltpu
from jax.sharding import PartitionSpec as P

BF = jnp.bfloat16
F32 = jnp.float32
TILE = 512


def iota(shape, axis):
    return lax.broadcasted_iota(jnp.int32, shape, axis)


def dot(left, right):
    return jnp.dot(left, right, preferred_element_type=F32)


def dot_cols(left, right):
    return lax.dot_general(left, right, (((1,), (1,)), ((), ())), preferred_element_type=F32)


def pick_ranks(experts_ref, count):
    first, second = experts_ref[0:1, :], experts_ref[1:2, :]
    toks = experts_ref.shape[1]
    names = iota((count, toks), 0)
    is_first, is_second = names == first, names == second
    either = jnp.where(is_first | is_second, 1.0, 0.0).astype(BF)
    earlier = jnp.where(iota((toks, toks), 0) < iota((toks, toks), 1), 1.0, 0.0).astype(BF)
    before = dot(either, earlier)
    ranks = [
        jnp.sum(jnp.where(mask, before, 0.0), axis=0, keepdims=True).astype(jnp.int32)
        for mask in (is_first, is_second)
    ]
    return ((first, ranks[0]), (second, ranks[1]))


def wide_row(expert, rank):
    return jnp.where(rank < 8, expert * 8 + rank, -1)


def half_row(expert, rank, half):
    return jnp.where(rank >= 8, expert * 8 + half * 4 + rank - 8, -1)


def as_column(row):
    toks = row.shape[1]
    eye = iota((toks, toks), 0) == iota((toks, toks), 1)
    return jnp.sum(jnp.where(eye, row, jnp.zeros_like(row)), axis=1, keepdims=True)


def send_masks(experts_ref, count):
    rows = count * 8
    toks = experts_ref.shape[1]
    row = iota((rows, toks), 0)
    out = []
    for expert, rank in pick_ranks(experts_ref, count):
        out.append(
            (
                row == wide_row(expert, rank),
                row == half_row(expert, rank, 0),
                row == half_row(expert, rank, 1),
            )
        )
    return out


def one_hot(*masks):
    both = masks[0]
    for mask in masks[1:]:
        both = both | mask
    return jnp.where(both, 1.0, 0.0).astype(BF)


def pack_tokens(experts_ref, rows_ref, out_ref):
    count = out_ref.shape[0] // 8
    width = rows_ref.shape[1]
    half = width // 2
    first, second = send_masks(experts_ref, count)
    wide = one_hot(first[0], second[0])
    halves = [one_hot(first[1 + h], second[1 + h]) for h in range(2)]
    for c in range(0, width, TILE):
        out_ref[:, c : c + TILE] = dot(wide, rows_ref[:, c : c + TILE]).astype(BF)
    for c in range(0, half, TILE):
        out_ref[:, width + c : width + c + TILE] = (
            dot(halves[0], rows_ref[:, c : c + TILE])
            + dot(halves[1], rows_ref[:, half + c : half + c + TILE])
        ).astype(BF)


def pack_grads(experts_ref, gates_ref, rows_ref, out_ref):
    count = out_ref.shape[0] // 8
    width = rows_ref.shape[1]
    half = width // 2
    first, second = send_masks(experts_ref, count)
    gate0, gate1 = gates_ref[0:1, :], gates_ref[1:2, :]

    def gate_of(mask0, mask1):
        return jnp.sum(
            jnp.where(mask0, gate0, 0.0) + jnp.where(mask1, gate1, 0.0), axis=1, keepdims=True
        )

    wide = one_hot(first[0], second[0])
    wide_gate = gate_of(first[0], second[0])
    halves = [one_hot(first[1 + h], second[1 + h]) for h in range(2)]
    half_gate = gate_of(first[1] | first[2], second[1] | second[2])
    for c in range(0, width, TILE):
        out_ref[:, c : c + TILE] = (wide_gate * dot(wide, rows_ref[:, c : c + TILE])).astype(BF)
    for c in range(0, half, TILE):
        out_ref[:, width + c : width + c + TILE] = (
            half_gate
            * (
                dot(halves[0], rows_ref[:, c : c + TILE])
                + dot(halves[1], rows_ref[:, half + c : half + c + TILE])
            )
        ).astype(BF)


def fetch_masks(experts_ref, count):
    rows = count * 8
    toks = experts_ref.shape[1]
    col = iota((toks, rows), 1)
    out = []
    for expert, rank in pick_ranks(experts_ref, count):
        targets = (wide_row(expert, rank), half_row(expert, rank, 0), half_row(expert, rank, 1))
        out.append(tuple(col == as_column(t) for t in targets))
    return out


def combine_out(experts_ref, gates_ref, got_ref, grad_ref, mixed_ref, gate_grad_ref):
    count = got_ref.shape[0] // 8
    toks, width = mixed_ref.shape
    half = width // 2
    masks = fetch_masks(experts_ref, count)
    wide = [one_hot(m[0]) for m in masks]
    halves = [[one_hot(m[1 + h]) for m in masks] for h in range(2)]
    gates = [as_column(gates_ref[k : k + 1, :]) for k in range(2)]
    sums = [jnp.zeros((toks, 1), F32) for _ in range(2)]
    for c in range(0, width, TILE):
        h, low = c // half, width + c % half
        grad = grad_ref[:, c : c + TILE].astype(F32)
        total = jnp.zeros((toks, TILE), F32)
        for k in range(2):
            picked = dot(wide[k], got_ref[:, c : c + TILE]) + dot(
                halves[h][k], got_ref[:, low : low + TILE]
            )
            total = total + gates[k] * picked
            sums[k] = sums[k] + jnp.sum(grad * picked, axis=1, keepdims=True)
        mixed_ref[:, c : c + TILE] = total.astype(BF)
    lane = iota((toks, 2), 1)
    gate_grad_ref[...] = jnp.where(lane == 0, sums[0], sums[1])


def combine_grads(experts_ref, got_ref, out_ref):
    count = got_ref.shape[0] // 8
    width = out_ref.shape[1]
    half = width // 2
    first, second = fetch_masks(experts_ref, count)
    wide = one_hot(first[0], second[0])
    halves = [one_hot(first[1 + h], second[1 + h]) for h in range(2)]
    for c in range(0, width, TILE):
        low = width + c % half
        out_ref[:, c : c + TILE] = (
            dot(wide, got_ref[:, c : c + TILE]) + dot(halves[c // half], got_ref[:, low : low + TILE])
        ).astype(BF)


def split_rows(got_ref, rows_ref):
    count = got_ref.shape[0]
    width = rows_ref.shape[1]
    half = width // 2
    tail = count // 2
    rows_ref[0:count, :] = got_ref[:, 0:width]
    row, col = iota((tail, count), 0), iota((tail, count), 1)
    for h in range(2):
        pick = one_hot(col == (row >> 2) * 8 + h * 4 + (row & 3))
        for c in range(0, half, TILE):
            rows_ref[count : count + tail, h * half + c : h * half + c + TILE] = dot(
                pick, got_ref[:, width + c : width + c + TILE]
            ).astype(BF)


def tail_spread(count):
    tail = count // 2
    row, col = iota((count, tail), 0), iota((count, tail), 1)
    return [one_hot(row == (col >> 2) * 8 + h * 4 + (col & 3)) for h in range(2)]


def store_rows(product, send_ref, tail_ref, width, at, size):
    count = send_ref.shape[0]
    send_ref[:, at : at + size] = product[0:count]
    tail_ref[:, at : at + size] = product[count:]


def flush_tail(send_ref, tail_ref, width):
    count = send_ref.shape[0]
    half = width // 2
    spread = tail_spread(count)
    for c in range(0, half, TILE):
        send_ref[:, width + c : width + c + TILE] = (
            dot(spread[0], tail_ref[:, c : c + TILE])
            + dot(spread[1], tail_ref[:, half + c : half + c + TILE])
        ).astype(BF)


def forward_rows(got_ref, weights_ref, send_ref, rows_ref, gate_ref, up_ref, hidden_ref, tail_ref):
    width = rows_ref.shape[1]
    hid = gate_ref.shape[1]
    split_rows(got_ref, rows_ref)
    for c in range(0, hid, 256):
        gate = dot(rows_ref[...], weights_ref[:, c : c + 256])
        up = dot(rows_ref[...], weights_ref[:, hid + c : hid + c + 256])
        gate_ref[:, c : c + 256] = gate
        up_ref[:, c : c + 256] = up
        hidden_ref[:, c : c + 256] = (gate * jax.nn.sigmoid(gate) * up).astype(BF)
    for c in range(0, width, 256):
        product = dot_cols(hidden_ref[...], weights_ref[c : c + 256, 2 * hid : 3 * hid]).astype(BF)
        store_rows(product, send_ref, tail_ref, width, c, 256)
    flush_tail(send_ref, tail_ref, width)


def backward_rows(got_ref, weights_ref, gate_ref, up_ref, send_ref, pre_ref, rows_ref, tail_ref):
    width = rows_ref.shape[1]
    hid = gate_ref.shape[1]
    split_rows(got_ref, rows_ref)
    for c in range(0, hid, 256):
        grad = dot(rows_ref[...], weights_ref[:, 2 * hid + c : 2 * hid + c + 256])
        gate, up = gate_ref[:, c : c + 256], up_ref[:, c : c + 256]
        sigma = jax.nn.sigmoid(gate)
        pre_ref[:, hid + c : hid + c + 256] = (grad * gate * sigma).astype(BF)
        pre_ref[:, c : c + 256] = (grad * up * sigma * (1.0 + gate * (1.0 - sigma))).astype(BF)
    for c in range(0, width, 256):
        product = dot_cols(pre_ref[...], weights_ref[c : c + 256, 0 : 2 * hid]).astype(BF)
        store_rows(product, send_ref, tail_ref, width, c, 256)
    flush_tail(send_ref, tail_ref, width)


def call(body, outs, scratch, flops, *args):
    size = sum(a.size * a.dtype.itemsize for a in args)
    size += sum(o[0][0] * o[0][1] * jnp.dtype(o[1]).itemsize for o in outs)
    return pl.pallas_call(
        body,
        out_shape=[jax.ShapeDtypeStruct(s, d) for s, d in outs],
        in_specs=[pl.BlockSpec(memory_space=pltpu.VMEM) for _ in args],
        out_specs=[pl.BlockSpec(memory_space=pltpu.VMEM) for _ in outs],
        scratch_shapes=[pltpu.VMEM(s, d) for s, d in scratch],
        cost_estimate=pl.CostEstimate(flops=flops, bytes_accessed=size, transcendentals=0),
        compiler_params=pltpu.CompilerParams(vmem_limit_bytes=12 << 20),
    )(*args)


def on_device(tokens, gates, experts, gate_weight, up_weight, down_weight, out_grad):
    toks, width = tokens.shape
    hid = gate_weight.shape[2]
    count = lax.axis_size("expert") * gate_weight.shape[0]
    send = (count * 8, 3 * width // 2)
    slots = count * 12
    experts_t, gates_t = experts.T, gates.T

    def exchange(rows):
        moved = lax.all_to_all(
            rows.reshape(count, 8, send[1]), "expert", split_axis=0, concat_axis=0, tiled=True
        )
        return moved.reshape(send)

    weights = lax.all_gather(
        jnp.concatenate([gate_weight, up_weight, down_weight], axis=2), "dp", axis=1, tiled=True
    )[0]
    pack_flops = 2 * send[0] * toks * send[1]
    (send_tok,) = call(pack_tokens, [(send, BF)], [], pack_flops, experts_t, tokens)
    (send_grad,) = call(pack_grads, [(send, BF)], [], pack_flops, experts_t, gates_t, out_grad)
    got_tok = exchange(send_tok)
    got_tok, send_grad = lax.optimization_barrier((got_tok, send_grad))
    got_grad = exchange(send_grad)
    send_out, rows_in, gate_pre, up_pre = call(
        forward_rows,
        [(send, BF), ((slots, width), BF), ((slots, hid), F32), ((slots, hid), F32)],
        [((slots, hid), BF), ((slots - send[0], width), BF)],
        6 * slots * width * hid,
        got_tok,
        weights,
    )
    got_grad, send_out = lax.optimization_barrier((got_grad, send_out))
    got_out = exchange(send_out)
    send_back, pre_grads = call(
        backward_rows,
        [(send, BF), ((slots, 2 * hid), BF)],
        [((slots, width), BF), ((slots - send[0], width), BF)],
        6 * slots * width * hid,
        got_grad,
        weights,
        gate_pre,
        up_pre,
    )
    partial = lax.dot_general(
        rows_in, pre_grads, (((0,), (0,)), ((), ())), preferred_element_type=F32
    )[None]
    summed = lax.psum_scatter(
        partial.astype(BF), "dp", scatter_dimension=1, tiled=True
    ).astype(F32)
    got_out, send_back = lax.optimization_barrier((got_out, send_back))
    got_back = exchange(send_back)
    mixed, gate_grad = call(
        combine_out,
        [((toks, width), BF), ((toks, 2), F32)],
        [],
        400 * toks * send[0] * width * 2,
        experts_t,
        gates_t,
        got_out,
        out_grad,
    )
    (token_grad,) = call(
        combine_grads, [((toks, width), BF)], [], 4 * toks * send[0] * width, experts_t, got_back
    )
    return (mixed, token_grad, gate_grad, summed[:, :, :hid], summed[:, :, hid:])


def solution(mesh):
    return jax.shard_map(
        on_device,
        mesh=mesh,
        in_specs=(
            P(("dp", "expert"), None),
            P(("dp", "expert"), None),
            P(("dp", "expert"), None),
            P("expert", "dp", None),
            P("expert", "dp", None),
            P("expert", "dp", None),
            P(("dp", "expert"), None),
        ),
        out_specs=(
            P(("dp", "expert"), None),
            P(("dp", "expert"), None),
            P(("dp", "expert"), None),
            P("expert", "dp", None),
            P("expert", "dp", None),
        ),
        check_vma=False,
    )
```

```python
import jax
import jax.numpy as jnp
from jax import lax
from jax.experimental import pallas as pl
from jax.experimental.pallas import tpu as pltpu
from jax.sharding import PartitionSpec as P

BF = jnp.bfloat16
F32 = jnp.float32
TILE = 512


def iota(shape, axis):
    return lax.broadcasted_iota(jnp.int32, shape, axis)


def dot(left, right):
    return jnp.dot(left, right, preferred_element_type=F32)


def dot_cols(left, right):
    return lax.dot_general(left, right, (((1,), (1,)), ((), ())), preferred_element_type=F32)


def turn(expert):
    return (expert & 3) * 8 + (expert >> 2)


def pick_ranks(experts_ref, count):
    first, second = turn(experts_ref[0:1, :]), turn(experts_ref[1:2, :])
    toks = experts_ref.shape[1]
    names = iota((count, toks), 0)
    is_first, is_second = names == first, names == second
    either = jnp.where(is_first | is_second, 1.0, 0.0).astype(BF)
    earlier = jnp.where(iota((toks, toks), 0) < iota((toks, toks), 1), 1.0, 0.0).astype(BF)
    before = dot(either, earlier)
    ranks = [
        jnp.sum(jnp.where(mask, before, 0.0), axis=0, keepdims=True).astype(jnp.int32)
        for mask in (is_first, is_second)
    ]
    return ((first, ranks[0]), (second, ranks[1]))


def wide_row(expert, rank):
    return jnp.where(rank < 8, expert * 8 + rank, -1)


def half_row(expert, rank, half):
    return jnp.where(rank >= 8, expert * 8 + half * 4 + rank - 8, -1)


def as_column(row):
    toks = row.shape[1]
    eye = iota((toks, toks), 0) == iota((toks, toks), 1)
    return jnp.sum(jnp.where(eye, row, jnp.zeros_like(row)), axis=1, keepdims=True)


def send_masks(experts_ref, count):
    rows = count * 8
    toks = experts_ref.shape[1]
    row = iota((rows, toks), 0)
    out = []
    for expert, rank in pick_ranks(experts_ref, count):
        out.append(
            (
                row == wide_row(expert, rank),
                row == half_row(expert, rank, 0),
                row == half_row(expert, rank, 1),
            )
        )
    return out


def one_hot(*masks):
    both = masks[0]
    for mask in masks[1:]:
        both = both | mask
    return jnp.where(both, 1.0, 0.0).astype(BF)


def pack_tokens(experts_ref, rows_ref, out_ref):
    count = out_ref.shape[0] // 8
    width = rows_ref.shape[1]
    half = width // 2
    first, second = send_masks(experts_ref, count)
    wide = one_hot(first[0], second[0])
    halves = [one_hot(first[1 + h], second[1 + h]) for h in range(2)]
    for c in range(0, width, TILE):
        out_ref[:, c : c + TILE] = dot(wide, rows_ref[:, c : c + TILE]).astype(BF)
    for c in range(0, half, TILE):
        out_ref[:, width + c : width + c + TILE] = (
            dot(halves[0], rows_ref[:, c : c + TILE])
            + dot(halves[1], rows_ref[:, half + c : half + c + TILE])
        ).astype(BF)


def pack_grads(experts_ref, gates_ref, rows_ref, out_ref):
    count = out_ref.shape[0] // 8
    width = rows_ref.shape[1]
    half = width // 2
    first, second = send_masks(experts_ref, count)
    gate0, gate1 = gates_ref[0:1, :], gates_ref[1:2, :]

    def gate_of(mask0, mask1):
        return jnp.sum(
            jnp.where(mask0, gate0, 0.0) + jnp.where(mask1, gate1, 0.0), axis=1, keepdims=True
        )

    wide = one_hot(first[0], second[0])
    wide_gate = gate_of(first[0], second[0])
    halves = [one_hot(first[1 + h], second[1 + h]) for h in range(2)]
    half_gate = gate_of(first[1] | first[2], second[1] | second[2])
    for c in range(0, width, TILE):
        out_ref[:, c : c + TILE] = (wide_gate * dot(wide, rows_ref[:, c : c + TILE])).astype(BF)
    for c in range(0, half, TILE):
        out_ref[:, width + c : width + c + TILE] = (
            half_gate
            * (
                dot(halves[0], rows_ref[:, c : c + TILE])
                + dot(halves[1], rows_ref[:, half + c : half + c + TILE])
            )
        ).astype(BF)


def fetch_masks(experts_ref, count):
    rows = count * 8
    toks = experts_ref.shape[1]
    col = iota((toks, rows), 1)
    out = []
    for expert, rank in pick_ranks(experts_ref, count):
        targets = (wide_row(expert, rank), half_row(expert, rank, 0), half_row(expert, rank, 1))
        out.append(tuple(col == as_column(t) for t in targets))
    return out


def combine_out(experts_ref, gates_ref, got_ref, grad_ref, mixed_ref, gate_grad_ref):
    count = got_ref.shape[0] // 8
    toks, width = mixed_ref.shape
    half = width // 2
    masks = fetch_masks(experts_ref, count)
    wide = [one_hot(m[0]) for m in masks]
    halves = [[one_hot(m[1 + h]) for m in masks] for h in range(2)]
    gates = [as_column(gates_ref[k : k + 1, :]) for k in range(2)]
    sums = [jnp.zeros((toks, 1), F32) for _ in range(2)]
    for c in range(0, width, TILE):
        h, low = c // half, width + c % half
        grad = grad_ref[:, c : c + TILE].astype(F32)
        total = jnp.zeros((toks, TILE), F32)
        for k in range(2):
            picked = dot(wide[k], got_ref[:, c : c + TILE]) + dot(
                halves[h][k], got_ref[:, low : low + TILE]
            )
            total = total + gates[k] * picked
            sums[k] = sums[k] + jnp.sum(grad * picked, axis=1, keepdims=True)
        mixed_ref[:, c : c + TILE] = total.astype(BF)
    lane = iota((toks, 2), 1)
    gate_grad_ref[...] = jnp.where(lane == 0, sums[0], sums[1])


def combine_grads(experts_ref, got_ref, out_ref):
    count = got_ref.shape[0] // 8
    width = out_ref.shape[1]
    half = width // 2
    first, second = fetch_masks(experts_ref, count)
    wide = one_hot(first[0], second[0])
    halves = [one_hot(first[1 + h], second[1 + h]) for h in range(2)]
    for c in range(0, width, TILE):
        low = width + c % half
        out_ref[:, c : c + TILE] = (
            dot(wide, got_ref[:, c : c + TILE]) + dot(halves[c // half], got_ref[:, low : low + TILE])
        ).astype(BF)


def split_rows(got_ref, rows_ref):
    count = got_ref.shape[0]
    width = rows_ref.shape[1]
    half = width // 2
    tail = count // 2
    rows_ref[0:count, :] = got_ref[:, 0:width]
    row, col = iota((tail, count), 0), iota((tail, count), 1)
    for h in range(2):
        pick = one_hot(col == (row >> 2) * 8 + h * 4 + (row & 3))
        for c in range(0, half, TILE):
            rows_ref[count : count + tail, h * half + c : h * half + c + TILE] = dot(
                pick, got_ref[:, width + c : width + c + TILE]
            ).astype(BF)


def tail_spread(count):
    tail = count // 2
    row, col = iota((count, tail), 0), iota((count, tail), 1)
    return [one_hot(row == (col >> 2) * 8 + h * 4 + (col & 3)) for h in range(2)]


def store_rows(product, send_ref, tail_ref, width, at, size):
    count = send_ref.shape[0]
    send_ref[:, at : at + size] = product[0:count]
    tail_ref[:, at : at + size] = product[count:]


def flush_tail(send_ref, tail_ref, width):
    count = send_ref.shape[0]
    half = width // 2
    spread = tail_spread(count)
    for c in range(0, half, TILE):
        send_ref[:, width + c : width + c + TILE] = (
            dot(spread[0], tail_ref[:, c : c + TILE])
            + dot(spread[1], tail_ref[:, half + c : half + c + TILE])
        ).astype(BF)


def forward_rows(got_ref, weights_ref, send_ref, rows_ref, gate_ref, up_ref, hidden_ref, tail_ref):
    width = rows_ref.shape[1]
    hid = gate_ref.shape[1]
    split_rows(got_ref, rows_ref)
    for c in range(0, hid, 256):
        gate = dot(rows_ref[...], weights_ref[:, c : c + 256])
        up = dot(rows_ref[...], weights_ref[:, hid + c : hid + c + 256])
        gate_ref[:, c : c + 256] = gate
        up_ref[:, c : c + 256] = up
        hidden_ref[:, c : c + 256] = (gate * jax.nn.sigmoid(gate) * up).astype(BF)
    for c in range(0, width, 256):
        product = dot_cols(hidden_ref[...], weights_ref[c : c + 256, 2 * hid : 3 * hid]).astype(BF)
        store_rows(product, send_ref, tail_ref, width, c, 256)
    flush_tail(send_ref, tail_ref, width)


def backward_rows(got_ref, weights_ref, gate_ref, up_ref, send_ref, pre_ref, rows_ref, tail_ref):
    width = rows_ref.shape[1]
    hid = gate_ref.shape[1]
    split_rows(got_ref, rows_ref)
    for c in range(0, hid, 256):
        grad = dot(rows_ref[...], weights_ref[:, 2 * hid + c : 2 * hid + c + 256])
        gate, up = gate_ref[:, c : c + 256], up_ref[:, c : c + 256]
        sigma = jax.nn.sigmoid(gate)
        pre_ref[:, hid + c : hid + c + 256] = (grad * gate * sigma).astype(BF)
        pre_ref[:, c : c + 256] = (grad * up * sigma * (1.0 + gate * (1.0 - sigma))).astype(BF)
    for c in range(0, width, 256):
        product = dot_cols(pre_ref[...], weights_ref[c : c + 256, 0 : 2 * hid]).astype(BF)
        store_rows(product, send_ref, tail_ref, width, c, 256)
    flush_tail(send_ref, tail_ref, width)


def call(body, outs, scratch, flops, *args):
    size = sum(a.size * a.dtype.itemsize for a in args)
    size += sum(o[0][0] * o[0][1] * jnp.dtype(o[1]).itemsize for o in outs)
    return pl.pallas_call(
        body,
        out_shape=[jax.ShapeDtypeStruct(s, d) for s, d in outs],
        in_specs=[pl.BlockSpec(memory_space=pltpu.VMEM) for _ in args],
        out_specs=[pl.BlockSpec(memory_space=pltpu.VMEM) for _ in outs],
        scratch_shapes=[pltpu.VMEM(s, d) for s, d in scratch],
        cost_estimate=pl.CostEstimate(flops=flops, bytes_accessed=size, transcendentals=0),
        compiler_params=pltpu.CompilerParams(vmem_limit_bytes=12 << 20),
    )(*args)


def on_device(tokens, gates, experts, gate_weight, up_weight, down_weight, out_grad):
    toks, width = tokens.shape
    hid = gate_weight.shape[2]
    count = lax.axis_size("expert") * gate_weight.shape[0]
    send = (count * 8, 3 * width // 2)
    slots = count * 12
    experts_t, gates_t = experts.T, gates.T

    def exchange(rows):
        moved = lax.all_to_all(
            rows.reshape(count, 8, send[1]),
            "expert",
            split_axis=0,
            concat_axis=0,
            tiled=True,
            axis_index_groups=[[y * 4 + x for x in range(4) for y in range(8)]],
        )
        return moved.reshape(send)

    pack_flops = 2 * send[0] * toks * send[1]
    (send_tok,) = call(pack_tokens, [(send, BF)], [], pack_flops, experts_t, tokens)
    shards, send_tok = lax.optimization_barrier(((gate_weight, up_weight, down_weight), send_tok))
    weights = lax.all_gather(jnp.concatenate(shards, axis=2), "dp", axis=1, tiled=True)[0]
    (send_grad,) = call(pack_grads, [(send, BF)], [], pack_flops, experts_t, gates_t, out_grad)
    got_tok = exchange(send_tok)
    got_tok, send_grad = lax.optimization_barrier((got_tok, send_grad))
    got_grad = exchange(send_grad)
    send_out, rows_in, gate_pre, up_pre = call(
        forward_rows,
        [(send, BF), ((slots, width), BF), ((slots, hid), F32), ((slots, hid), F32)],
        [((slots, hid), BF), ((slots - send[0], width), BF)],
        6 * slots * width * hid,
        got_tok,
        weights,
    )
    got_grad, send_out = lax.optimization_barrier((got_grad, send_out))
    got_out = exchange(send_out)
    send_back, pre_grads = call(
        backward_rows,
        [(send, BF), ((slots, 2 * hid), BF)],
        [((slots, width), BF), ((slots - send[0], width), BF)],
        6 * slots * width * hid,
        got_grad,
        weights,
        gate_pre,
        up_pre,
    )
    partial = lax.dot_general(
        rows_in, pre_grads, (((0,), (0,)), ((), ())), preferred_element_type=F32
    )[None]
    summed = lax.psum_scatter(
        partial.astype(BF), "dp", scatter_dimension=1, tiled=True
    ).astype(F32)
    got_out, send_back = lax.optimization_barrier((got_out, send_back))
    got_back = exchange(send_back)
    mixed, gate_grad = call(
        combine_out,
        [((toks, width), BF), ((toks, 2), F32)],
        [],
        40000000 * toks * send[0] * width * 2,
        experts_t,
        gates_t,
        got_out,
        out_grad,
    )
    got_back, summed = lax.optimization_barrier((got_back, (summed[:, :, :hid], summed[:, :, hid:])))
    (token_grad,) = call(
        combine_grads, [((toks, width), BF)], [], 4 * toks * send[0] * width, experts_t, got_back
    )
    return (mixed, token_grad, gate_grad, *summed)


def solution(mesh):
    return jax.shard_map(
        on_device,
        mesh=mesh,
        in_specs=(
            P(("dp", "expert"), None),
            P(("dp", "expert"), None),
            P(("dp", "expert"), None),
            P("expert", "dp", None),
            P("expert", "dp", None),
            P("expert", "dp", None),
            P(("dp", "expert"), None),
        ),
        out_specs=(
            P(("dp", "expert"), None),
            P(("dp", "expert"), None),
            P(("dp", "expert"), None),
            P("expert", "dp", None),
            P("expert", "dp", None),
        ),
        check_vma=False,
    )
```

```python
import functools

import jax
import jax.numpy as jnp
from jax import lax
from jax.experimental import pallas as pl
from jax.experimental.pallas import tpu as pltpu
from jax.sharding import PartitionSpec as P

BF = jnp.bfloat16
F32 = jnp.float32
TILE = 512


def iota(shape, axis):
    return lax.broadcasted_iota(jnp.int32, shape, axis)


def dot(left, right):
    return jnp.dot(left, right, preferred_element_type=F32)


def dot_cols(left, right):
    return lax.dot_general(left, right, (((1,), (1,)), ((), ())), preferred_element_type=F32)


def turn(expert):
    return (expert & 3) * 8 + (expert >> 2)


def pick_ranks(experts_ref, count):
    first, second = turn(experts_ref[0:1, :]), turn(experts_ref[1:2, :])
    toks = experts_ref.shape[1]
    names = iota((count, toks), 0)
    is_first, is_second = names == first, names == second
    either = jnp.where(is_first | is_second, 1.0, 0.0).astype(BF)
    earlier = jnp.where(iota((toks, toks), 0) < iota((toks, toks), 1), 1.0, 0.0).astype(BF)
    before = dot(either, earlier)
    ranks = [
        jnp.sum(jnp.where(mask, before, 0.0), axis=0, keepdims=True).astype(jnp.int32)
        for mask in (is_first, is_second)
    ]
    return ((first, ranks[0]), (second, ranks[1]))


def wide_row(expert, rank):
    return jnp.where(rank < 8, expert * 8 + rank, -1)


def half_row(expert, rank, half):
    return jnp.where(rank >= 8, expert * 8 + half * 4 + rank - 8, -1)


def as_column(row):
    toks = row.shape[1]
    eye = iota((toks, toks), 0) == iota((toks, toks), 1)
    return jnp.sum(jnp.where(eye, row, jnp.zeros_like(row)), axis=1, keepdims=True)


def send_masks(experts_ref, count):
    rows = count * 8
    toks = experts_ref.shape[1]
    row = iota((rows, toks), 0)
    out = []
    for expert, rank in pick_ranks(experts_ref, count):
        out.append(
            (
                row == wide_row(expert, rank),
                row == half_row(expert, rank, 0),
                row == half_row(expert, rank, 1),
            )
        )
    return out


def one_hot(*masks):
    both = masks[0]
    for mask in masks[1:]:
        both = both | mask
    return jnp.where(both, 1.0, 0.0).astype(BF)


def pack_tokens(experts_ref, rows_ref, out_ref):
    count = out_ref.shape[0] // 8
    width = rows_ref.shape[1]
    half = width // 2
    first, second = send_masks(experts_ref, count)
    wide = one_hot(first[0], second[0])
    halves = [one_hot(first[1 + h], second[1 + h]) for h in range(2)]
    for c in range(0, width, TILE):
        out_ref[:, c : c + TILE] = dot(wide, rows_ref[:, c : c + TILE]).astype(BF)
    for c in range(0, half, TILE):
        out_ref[:, width + c : width + c + TILE] = (
            dot(halves[0], rows_ref[:, c : c + TILE])
            + dot(halves[1], rows_ref[:, half + c : half + c + TILE])
        ).astype(BF)


def pack_grads(experts_ref, gates_ref, rows_ref, out_ref):
    count = out_ref.shape[0] // 8
    width = rows_ref.shape[1]
    half = width // 2
    first, second = send_masks(experts_ref, count)
    gate0, gate1 = gates_ref[0:1, :], gates_ref[1:2, :]

    def gate_of(mask0, mask1):
        return jnp.sum(
            jnp.where(mask0, gate0, 0.0) + jnp.where(mask1, gate1, 0.0), axis=1, keepdims=True
        )

    wide = one_hot(first[0], second[0])
    wide_gate = gate_of(first[0], second[0])
    halves = [one_hot(first[1 + h], second[1 + h]) for h in range(2)]
    half_gate = gate_of(first[1] | first[2], second[1] | second[2])
    for c in range(0, width, TILE):
        out_ref[:, c : c + TILE] = (wide_gate * dot(wide, rows_ref[:, c : c + TILE])).astype(BF)
    for c in range(0, half, TILE):
        out_ref[:, width + c : width + c + TILE] = (
            half_gate
            * (
                dot(halves[0], rows_ref[:, c : c + TILE])
                + dot(halves[1], rows_ref[:, half + c : half + c + TILE])
            )
        ).astype(BF)


def fetch_masks(experts_ref, count):
    rows = count * 8
    toks = experts_ref.shape[1]
    col = iota((toks, rows), 1)
    out = []
    for expert, rank in pick_ranks(experts_ref, count):
        targets = (wide_row(expert, rank), half_row(expert, rank, 0), half_row(expert, rank, 1))
        out.append(tuple(col == as_column(t) for t in targets))
    return out


def combine_out(experts_ref, gates_ref, got_ref, grad_ref, mixed_ref, gate_grad_ref):
    count = got_ref.shape[0] // 8
    toks, width = mixed_ref.shape
    half = width // 2
    masks = fetch_masks(experts_ref, count)
    wide = [one_hot(m[0]) for m in masks]
    halves = [[one_hot(m[1 + h]) for m in masks] for h in range(2)]
    gates = [as_column(gates_ref[k : k + 1, :]) for k in range(2)]
    sums = [jnp.zeros((toks, 1), F32) for _ in range(2)]
    for c in range(0, width, TILE):
        h, low = c // half, width + c % half
        grad = grad_ref[:, c : c + TILE].astype(F32)
        total = jnp.zeros((toks, TILE), F32)
        for k in range(2):
            picked = dot(wide[k], got_ref[:, c : c + TILE]) + dot(
                halves[h][k], got_ref[:, low : low + TILE]
            )
            total = total + gates[k] * picked
            sums[k] = sums[k] + jnp.sum(grad * picked, axis=1, keepdims=True)
        mixed_ref[:, c : c + TILE] = total.astype(BF)
    lane = iota((toks, 2), 1)
    gate_grad_ref[...] = jnp.where(lane == 0, sums[0], sums[1])


def combine_grads(experts_ref, got_ref, out_ref):
    count = got_ref.shape[0] // 8
    width = out_ref.shape[1]
    half = width // 2
    first, second = fetch_masks(experts_ref, count)
    wide = one_hot(first[0], second[0])
    halves = [one_hot(first[1 + h], second[1 + h]) for h in range(2)]
    for c in range(0, width, TILE):
        low = width + c % half
        out_ref[:, c : c + TILE] = (
            dot(wide, got_ref[:, c : c + TILE]) + dot(halves[c // half], got_ref[:, low : low + TILE])
        ).astype(BF)


def split_rows(got_ref, rows_ref):
    count = got_ref.shape[0]
    width = rows_ref.shape[1]
    half = width // 2
    tail = count // 2
    rows_ref[0:count, :] = got_ref[:, 0:width]
    row, col = iota((tail, count), 0), iota((tail, count), 1)
    for h in range(2):
        pick = one_hot(col == (row >> 2) * 8 + h * 4 + (row & 3))
        for c in range(0, half, TILE):
            rows_ref[count : count + tail, h * half + c : h * half + c + TILE] = dot(
                pick, got_ref[:, width + c : width + c + TILE]
            ).astype(BF)


def tail_spread(count):
    tail = count // 2
    row, col = iota((count, tail), 0), iota((count, tail), 1)
    return [one_hot(row == (col >> 2) * 8 + h * 4 + (col & 3)) for h in range(2)]


def store_rows(product, send_ref, tail_ref, width, at, size):
    count = send_ref.shape[0]
    send_ref[:, at : at + size] = product[0:count]
    tail_ref[:, at : at + size] = product[count:]


def flush_tail(send_ref, tail_ref, width):
    count = send_ref.shape[0]
    half = width // 2
    spread = tail_spread(count)
    for c in range(0, half, TILE):
        send_ref[:, width + c : width + c + TILE] = (
            dot(spread[0], tail_ref[:, c : c + TILE])
            + dot(spread[1], tail_ref[:, half + c : half + c + TILE])
        ).astype(BF)


def forward_rows(
    block, core_ref, got_ref, weights_ref, send_ref, turned_ref, gate_ref, up_ref, rows_ref, hidden_ref, tail_ref
):
    width = rows_ref.shape[1]
    hid = gate_ref.shape[1]
    split_rows(got_ref, rows_ref)
    for c in range(0, hid, 256):
        gate = dot(rows_ref[...], weights_ref[:, c : c + 256])
        up = dot(rows_ref[...], weights_ref[:, hid + c : hid + c + 256])
        gate_ref[:, c : c + 256] = gate
        up_ref[:, c : c + 256] = up
        hidden_ref[:, c : c + 256] = (gate * jax.nn.sigmoid(gate) * up).astype(BF)
    for c in range(0, width, 256):
        product = dot_cols(hidden_ref[...], weights_ref[c : c + 256, 2 * hid : 3 * hid]).astype(BF)
        store_rows(product, send_ref, tail_ref, width, c, 256)
    flush_tail(send_ref, tail_ref, width)
    core = core_ref[0]
    for side, owner in enumerate((core, 1 - core)):
        for c in range(0, width // 2, block):
            at = pl.multiple_of(2 * c + owner * block, 128)
            to = side * (width // 2) + c
            turned_ref[:, to : to + block] = rows_ref[:, pl.ds(at, block)]


def backward_hidden(
    got_ref, weights_ref, gate_ref, up_ref, turned_ref,
    pre_ref, keep_ref, give_ref,
    rows_ref, down_in, gate_in, up_in, turned_in, sums_ref, sems, out_sems,
):
    width = rows_ref.shape[1]
    hid = gate_ref.shape[1]
    copies = [
        pltpu.make_async_copy(source, target, sems.at[i])
        for i, (source, target) in enumerate(
            (
                (weights_ref.at[:, pl.ds(2 * hid, hid)], down_in),
                (gate_ref, gate_in),
                (up_ref, up_in),
                (turned_ref, turned_in),
            )
        )
    ]
    for copy in copies:
        copy.start()
    split_rows(got_ref, rows_ref)
    for copy in copies[:3]:
        copy.wait()
    for c in range(0, hid, 256):
        grad = dot(rows_ref[...], down_in[:, c : c + 256])
        gate, up = gate_in[:, c : c + 256], up_in[:, c : c + 256]
        sigma = jax.nn.sigmoid(gate)
        pre_ref[:, hid + c : hid + c + 256] = (grad * gate * sigma).astype(BF)
        pre_ref[:, c : c + 256] = (grad * up * sigma * (1.0 + gate * (1.0 - sigma))).astype(BF)
    copies[3].wait()
    leaving = []
    for side, out_ref in ((1, give_ref), (0, keep_ref)):
        for c in range(0, width // 2, 256):
            at = side * (width // 2) + c
            sums_ref[at : at + 256, :] = lax.dot_general(
                turned_in[:, at : at + 256],
                pre_ref[...],
                (((0,), (0,)), ((), ())),
                preferred_element_type=F32,
            ).astype(BF)
            leaving.append(
                pltpu.make_async_copy(
                    sums_ref.at[pl.ds(at, 256)], out_ref.at[pl.ds(c, 256)], out_sems.at[at // 256]
                )
            )
            leaving[-1].start()
    for copy in leaving:
        copy.wait()


def backward_rows(pre_ref, weights_ref, send_ref, both_in, tail_ref, sems):
    width = weights_ref.shape[0]
    both = pre_ref.shape[1]
    parts = 4
    size = width // parts
    copies = [
        pltpu.make_async_copy(
            weights_ref.at[pl.ds(i * size, size), pl.ds(0, both)],
            both_in.at[pl.ds(i * size, size)],
            sems.at[i],
        )
        for i in range(parts)
    ]
    for copy in copies:
        copy.start()
    for i in range(parts):
        copies[i].wait()
        for c in range(i * size, (i + 1) * size, 256):
            product = dot_cols(pre_ref[...], both_in[c : c + 256, :]).astype(BF)
            store_rows(product, send_ref, tail_ref, width, c, 256)
    flush_tail(send_ref, tail_ref, width)


def call(body, outs, scratch, flops, *args, far=(), far_outs=(), scalars=()):
    size = sum(a.size * a.dtype.itemsize for a in args)
    size += sum(o[0][0] * o[0][1] * jnp.dtype(o[1]).itemsize for o in outs)
    spaces = [
        pltpu.HBM if i in far else pltpu.SMEM if i in scalars else pltpu.VMEM for i in range(len(args))
    ]
    held = [pltpu.VMEM(*s) for s in scratch]
    if far:
        held.append(pltpu.SemaphoreType.DMA((4,)))
    if far_outs:
        held.append(pltpu.SemaphoreType.DMA((8,)))
    return pl.pallas_call(
        body,
        out_shape=[jax.ShapeDtypeStruct(s, d) for s, d in outs],
        in_specs=[pl.BlockSpec(memory_space=space) for space in spaces],
        out_specs=[
            pl.BlockSpec(memory_space=pltpu.HBM if i in far_outs else pltpu.VMEM)
            for i in range(len(outs))
        ],
        scratch_shapes=held,
        cost_estimate=pl.CostEstimate(flops=flops, bytes_accessed=size, transcendentals=0),
        compiler_params=pltpu.CompilerParams(vmem_limit_bytes=(58 if far else 12) << 20),
    )(*args)


def on_device(tokens, gates, experts, gate_weight, up_weight, down_weight, out_grad):
    toks, width = tokens.shape
    hid = gate_weight.shape[2]
    count = lax.axis_size("expert") * gate_weight.shape[0]
    send = (count * 8, 3 * width // 2)
    slots = count * 12
    experts_t, gates_t = experts.T, gates.T

    def exchange(rows):
        moved = lax.all_to_all(
            rows.reshape(count, 8, send[1]),
            "expert",
            split_axis=0,
            concat_axis=0,
            tiled=True,
            axis_index_groups=[[y * 4 + x for x in range(4) for y in range(8)]],
        )
        return moved.reshape(send)

    pack_flops = 2 * send[0] * toks * send[1]
    (send_tok,) = call(pack_tokens, [(send, BF)], [], pack_flops, experts_t, tokens)
    shards, send_tok = lax.optimization_barrier(((gate_weight, up_weight, down_weight), send_tok))
    weights = lax.all_gather(jnp.concatenate(shards, axis=2), "dp", axis=1, tiled=True)[0]
    (send_grad,) = call(pack_grads, [(send, BF)], [], pack_flops, experts_t, gates_t, out_grad)
    got_tok = exchange(send_tok)
    got_tok, send_grad = lax.optimization_barrier((got_tok, send_grad))
    got_grad = exchange(send_grad)
    core = (lax.axis_index("dp") % 2).astype(jnp.int32)[None]
    send_out, turned, gate_pre, up_pre = call(
        functools.partial(forward_rows, width // lax.axis_size("dp")),
        [(send, BF), ((slots, width), BF), ((slots, hid), F32), ((slots, hid), F32)],
        [((slots, width), BF), ((slots, hid), BF), ((slots - send[0], width), BF)],
        6 * slots * width * hid,
        core,
        got_tok,
        weights,
        scalars=(0,),
    )
    got_grad, send_out = lax.optimization_barrier((got_grad, send_out))
    got_out = exchange(send_out)
    half = (width // 2, 2 * hid)
    pre_grads, keep, give = call(
        backward_hidden,
        [((slots, 2 * hid), BF), (half, BF), (half, BF)],
        [
            ((slots, width), BF),
            ((width, hid), BF),
            ((slots, hid), F32),
            ((slots, hid), F32),
            ((slots, width), BF),
            ((width, 2 * hid), BF),
        ],
        6 * slots * width * hid,
        got_grad,
        weights,
        gate_pre,
        up_pre,
        turned,
        far=(1, 2, 3, 4),
        far_outs=(1, 2),
    )
    dp = lax.axis_size("dp")
    taken = lax.ppermute(give, "dp", [(i, i ^ 1) for i in range(dp)])
    pair = (keep.astype(F32) + taken.astype(F32)).astype(BF)
    summed = lax.psum_scatter(
        pair,
        "dp",
        scatter_dimension=0,
        tiled=True,
        axis_index_groups=[[i + c for i in range(0, dp, 2)] for c in range(2)],
    ).astype(F32)[None]
    (send_back,) = call(
        backward_rows,
        [(send, BF)],
        [((width, 2 * hid), BF), ((slots - send[0], width), BF)],
        4 * slots * width * hid,
        pre_grads,
        weights,
        far=(1,),
    )
    got_out, send_back = lax.optimization_barrier((got_out, send_back))
    got_back = exchange(send_back)
    mixed, gate_grad = call(
        combine_out,
        [((toks, width), BF), ((toks, 2), F32)],
        [],
        40000000 * toks * send[0] * width * 2,
        experts_t,
        gates_t,
        got_out,
        out_grad,
    )
    experts_t, summed = lax.optimization_barrier(
        (experts_t, (summed[:, :, :hid], summed[:, :, hid:]))
    )
    (token_grad,) = call(
        combine_grads, [((toks, width), BF)], [], 4 * toks * send[0] * width, experts_t, got_back
    )
    return (mixed, token_grad, gate_grad, *summed)


def solution(mesh):
    return jax.shard_map(
        on_device,
        mesh=mesh,
        in_specs=(
            P(("dp", "expert"), None),
            P(("dp", "expert"), None),
            P(("dp", "expert"), None),
            P("expert", "dp", None),
            P("expert", "dp", None),
            P("expert", "dp", None),
            P(("dp", "expert"), None),
        ),
        out_specs=(
            P(("dp", "expert"), None),
            P(("dp", "expert"), None),
            P(("dp", "expert"), None),
            P("expert", "dp", None),
            P("expert", "dp", None),
        ),
        check_vma=False,
    )
```

```python
import functools

import jax
import jax.numpy as jnp
from jax import lax
from jax.experimental import pallas as pl
from jax.experimental.pallas import tpu as pltpu
from jax.sharding import PartitionSpec as P

BF = jnp.bfloat16
F32 = jnp.float32
TILE = 512
AXIS = {}
EARLY = (3, 4, 5)


def iota(shape, axis):
    return lax.broadcasted_iota(jnp.int32, shape, axis)


def dot(left, right):
    return jnp.dot(left, right, preferred_element_type=F32)


def dot_cols(left, right):
    return lax.dot_general(left, right, (((1,), (1,)), ((), ())), preferred_element_type=F32)


def turn(expert):
    return (expert & 3) * 8 + (expert >> 2)


def pick_ranks(experts_ref, count):
    first, second = turn(experts_ref[0:1, :]), turn(experts_ref[1:2, :])
    toks = experts_ref.shape[1]
    names = iota((count, toks), 0)
    is_first, is_second = names == first, names == second
    either = jnp.where(is_first | is_second, 1.0, 0.0).astype(BF)
    earlier = jnp.where(iota((toks, toks), 0) < iota((toks, toks), 1), 1.0, 0.0).astype(BF)
    before = dot(either, earlier)
    ranks = [
        jnp.sum(jnp.where(mask, before, 0.0), axis=0, keepdims=True).astype(jnp.int32)
        for mask in (is_first, is_second)
    ]
    return ((first, ranks[0]), (second, ranks[1]))


def wide_row(expert, rank):
    return jnp.where(rank < 8, expert * 8 + rank, -1)


def half_row(expert, rank, half):
    return jnp.where(rank >= 8, expert * 8 + half * 4 + rank - 8, -1)


def as_column(row):
    toks = row.shape[1]
    eye = iota((toks, toks), 0) == iota((toks, toks), 1)
    return jnp.sum(jnp.where(eye, row, jnp.zeros_like(row)), axis=1, keepdims=True)


def send_masks(experts_ref, count):
    rows = count * 8
    toks = experts_ref.shape[1]
    row = iota((rows, toks), 0)
    out = []
    for expert, rank in pick_ranks(experts_ref, count):
        out.append(
            (
                row == wide_row(expert, rank),
                row == half_row(expert, rank, 0),
                row == half_row(expert, rank, 1),
            )
        )
    return out


def one_hot(*masks):
    both = masks[0]
    for mask in masks[1:]:
        both = both | mask
    return jnp.where(both, 1.0, 0.0).astype(BF)


def pack_tokens(experts_ref, rows_ref, out_ref):
    count = out_ref.shape[0] // 8
    width = rows_ref.shape[1]
    half = width // 2
    first, second = send_masks(experts_ref, count)
    wide = one_hot(first[0], second[0])
    halves = [one_hot(first[1 + h], second[1 + h]) for h in range(2)]
    for c in range(0, width, TILE):
        out_ref[:, c : c + TILE] = dot(wide, rows_ref[:, c : c + TILE]).astype(BF)
    for c in range(0, half, TILE):
        out_ref[:, width + c : width + c + TILE] = (
            dot(halves[0], rows_ref[:, c : c + TILE])
            + dot(halves[1], rows_ref[:, half + c : half + c + TILE])
        ).astype(BF)


def pack_grads(experts_ref, gates_ref, rows_ref, out_ref):
    count = out_ref.shape[0] // 8
    width = rows_ref.shape[1]
    half = width // 2
    first, second = send_masks(experts_ref, count)
    gate0, gate1 = gates_ref[0:1, :], gates_ref[1:2, :]

    def gate_of(mask0, mask1):
        return jnp.sum(
            jnp.where(mask0, gate0, 0.0) + jnp.where(mask1, gate1, 0.0), axis=1, keepdims=True
        )

    wide = one_hot(first[0], second[0])
    wide_gate = gate_of(first[0], second[0])
    halves = [one_hot(first[1 + h], second[1 + h]) for h in range(2)]
    half_gate = gate_of(first[1] | first[2], second[1] | second[2])
    for c in range(0, width, TILE):
        out_ref[:, c : c + TILE] = (wide_gate * dot(wide, rows_ref[:, c : c + TILE])).astype(BF)
    for c in range(0, half, TILE):
        out_ref[:, width + c : width + c + TILE] = (
            half_gate
            * (
                dot(halves[0], rows_ref[:, c : c + TILE])
                + dot(halves[1], rows_ref[:, half + c : half + c + TILE])
            )
        ).astype(BF)


def fetch_masks(experts_ref, count):
    rows = count * 8
    toks = experts_ref.shape[1]
    col = iota((toks, rows), 1)
    out = []
    for expert, rank in pick_ranks(experts_ref, count):
        targets = (wide_row(expert, rank), half_row(expert, rank, 0), half_row(expert, rank, 1))
        out.append(tuple(col == as_column(t) for t in targets))
    return out


def combine_out(experts_ref, gates_ref, got_ref, grad_ref, mixed_ref, gate_grad_ref):
    count = got_ref.shape[0] // 8
    toks, width = mixed_ref.shape
    half = width // 2
    masks = fetch_masks(experts_ref, count)
    wide = [one_hot(m[0]) for m in masks]
    halves = [[one_hot(m[1 + h]) for m in masks] for h in range(2)]
    gates = [as_column(gates_ref[k : k + 1, :]) for k in range(2)]
    sums = [jnp.zeros((toks, 1), F32) for _ in range(2)]
    for c in range(0, width, TILE):
        h, low = c // half, width + c % half
        grad = grad_ref[:, c : c + TILE].astype(F32)
        total = jnp.zeros((toks, TILE), F32)
        for k in range(2):
            picked = dot(wide[k], got_ref[:, c : c + TILE]) + dot(
                halves[h][k], got_ref[:, low : low + TILE]
            )
            total = total + gates[k] * picked
            sums[k] = sums[k] + jnp.sum(grad * picked, axis=1, keepdims=True)
        mixed_ref[:, c : c + TILE] = total.astype(BF)
    lane = iota((toks, 2), 1)
    gate_grad_ref[...] = jnp.where(lane == 0, sums[0], sums[1])


def combine_grads(experts_ref, got_ref, out_ref):
    count = got_ref.shape[0] // 8
    width = out_ref.shape[1]
    half = width // 2
    first, second = fetch_masks(experts_ref, count)
    wide = one_hot(first[0], second[0])
    halves = [one_hot(first[1 + h], second[1 + h]) for h in range(2)]
    for c in range(0, width, TILE):
        low = width + c % half
        out_ref[:, c : c + TILE] = (
            dot(wide, got_ref[:, c : c + TILE]) + dot(halves[c // half], got_ref[:, low : low + TILE])
        ).astype(BF)


def turned_blocks(place_ref, width, size):
    z, core = place_ref[0], place_ref[1]
    chips = AXIS["dp"] // 2
    block = width // (2 * chips)
    size = min(size, block)
    pairs = []
    for side, owner in enumerate((core, 1 - core)):
        for k in range(chips):
            shard = 2 * lax.rem(z + (chips - k), chips) + owner
            for c in range(0, block, size):
                column = pl.multiple_of(shard * block + c, 128)
                pairs.append((side * (width // 2) + k * block + c, column))
    return size, pairs


def split_rows(place_ref, got_ref, rows_ref, tail_ref):
    count = got_ref.shape[0]
    width = rows_ref.shape[1]
    half = width // 2
    tail = count // 2
    row, col = iota((tail, count), 0), iota((tail, count), 1)
    for h in range(2):
        pick = one_hot(col == (row >> 2) * 8 + h * 4 + (row & 3))
        for c in range(0, half, TILE):
            tail_ref[:, h * half + c : h * half + c + TILE] = dot(
                pick, got_ref[:, width + c : width + c + TILE]
            ).astype(BF)
    size, pairs = turned_blocks(place_ref, width, TILE)
    for to, column in pairs:
        rows_ref[0:count, to : to + size] = got_ref[:, pl.ds(column, size)]
        rows_ref[count:, to : to + size] = tail_ref[:, pl.ds(column, size)]


def tail_spread(count):
    tail = count // 2
    row, col = iota((count, tail), 0), iota((count, tail), 1)
    return [one_hot(row == (col >> 2) * 8 + h * 4 + (col & 3)) for h in range(2)]


def store_rows(place_ref, product, send_ref, tail_ref, width, at):
    count = send_ref.shape[0]
    size, pairs = turned_blocks(place_ref, width, 256)
    for to, column in pairs:
        if at <= to < at + 256:
            send_ref[:, pl.ds(column, size)] = product[0:count, to - at : to - at + size]
            tail_ref[:, pl.ds(column, size)] = product[count:, to - at : to - at + size]


def flush_tail(send_ref, tail_ref, width):
    count = send_ref.shape[0]
    half = width // 2
    spread = tail_spread(count)
    for c in range(0, half, TILE):
        send_ref[:, width + c : width + c + TILE] = (
            dot(spread[0], tail_ref[:, c : c + TILE])
            + dot(spread[1], tail_ref[:, half + c : half + c + TILE])
        ).astype(BF)


def dot_turned(rows_ref, mine_ref, other_ref, columns):
    half = mine_ref.shape[0]
    return dot(rows_ref[:, 0:half], mine_ref[:, columns]) + dot(
        rows_ref[:, half:], other_ref[:, columns]
    )


def forward_rows(
    place_ref, got_ref, mine_ref, other_ref, send_ref, rows_ref, gate_ref, up_ref, hidden_ref, tail_ref
):
    width = rows_ref.shape[1]
    half = width // 2
    hid = gate_ref.shape[1]
    split_rows(place_ref, got_ref, rows_ref, tail_ref)
    for c in range(0, hid, 256):
        gate = dot_turned(rows_ref, mine_ref, other_ref, slice(c, c + 256))
        up = dot_turned(rows_ref, mine_ref, other_ref, slice(hid + c, hid + c + 256))
        gate_ref[:, c : c + 256] = gate
        up_ref[:, c : c + 256] = up
        hidden_ref[:, c : c + 256] = (gate * jax.nn.sigmoid(gate) * up).astype(BF)
    for side, weights_ref in enumerate((mine_ref, other_ref)):
        for c in range(0, half, 256):
            product = dot_cols(hidden_ref[...], weights_ref[c : c + 256, 2 * hid : 3 * hid])
            store_rows(place_ref, product.astype(BF), send_ref, tail_ref, width, side * half + c)
    flush_tail(send_ref, tail_ref, width)


def backward_hidden(
    place_ref, got_ref, mine_ref, other_ref, gate_ref, up_ref, turned_ref,
    pre_ref, keep_ref, give_ref,
    rows_ref, mine_in, other_in, gate_in, up_in, turned_in, sums_ref, tail_ref, sems, out_sems,
):
    width = rows_ref.shape[1]
    hid = gate_ref.shape[1]
    copies = [
        pltpu.make_async_copy(source, target, sems.at[i])
        for i, (source, target) in enumerate(
            (
                (mine_ref.at[:, pl.ds(2 * hid, hid)], mine_in),
                (other_ref.at[:, pl.ds(2 * hid, hid)], other_in),
                (gate_ref, gate_in),
                (up_ref, up_in),
                (turned_ref, turned_in),
            )
        )
    ]
    for copy in copies:
        copy.start()
    split_rows(place_ref, got_ref, rows_ref, tail_ref)
    for copy in copies[:4]:
        copy.wait()
    for c in range(0, hid, 256):
        grad = dot_turned(rows_ref, mine_in, other_in, slice(c, c + 256))
        gate, up = gate_in[:, c : c + 256], up_in[:, c : c + 256]
        sigma = jax.nn.sigmoid(gate)
        pre_ref[:, hid + c : hid + c + 256] = (grad * gate * sigma).astype(BF)
        pre_ref[:, c : c + 256] = (grad * up * sigma * (1.0 + gate * (1.0 - sigma))).astype(BF)
    copies[4].wait()
    leaving = []
    for side, out_ref in ((1, give_ref), (0, keep_ref)):
        for c in range(0, width // 2, 256):
            at = side * (width // 2) + c
            sums_ref[at : at + 256, :] = lax.dot_general(
                turned_in[:, at : at + 256],
                pre_ref[...],
                (((0,), (0,)), ((), ())),
                preferred_element_type=F32,
            ).astype(BF)
            leaving.append(
                pltpu.make_async_copy(
                    sums_ref.at[pl.ds(at, 256)], out_ref.at[pl.ds(c, 256)], out_sems.at[at // 256]
                )
            )
            leaving[-1].start()
    for copy in leaving:
        copy.wait()


def backward_rows(place_ref, pre_ref, mine_ref, other_ref, send_ref, both_in, tail_ref, sems):
    half = mine_ref.shape[0]
    both = pre_ref.shape[1]
    size = half // 2
    copies = []
    for i in range(4):
        source = (mine_ref, other_ref)[i // 2]
        copies.append(
            pltpu.make_async_copy(
                source.at[pl.ds(i % 2 * size, size), pl.ds(0, both)],
                both_in.at[pl.ds(i * size, size)],
                sems.at[i],
            )
        )
        copies[-1].start()
    for i in range(4):
        copies[i].wait()
        for c in range(i * size, (i + 1) * size, 256):
            product = dot_cols(pre_ref[...], both_in[c : c + 256, :]).astype(BF)
            store_rows(place_ref, product, send_ref, tail_ref, 2 * half, c)
    flush_tail(send_ref, tail_ref, 2 * half)


def call(body, outs, scratch, flops, *args, far=(), far_outs=(), scalars=()):
    size = sum(a.size * a.dtype.itemsize for a in args)
    size += sum(o[0][0] * o[0][1] * jnp.dtype(o[1]).itemsize for o in outs)
    spaces = [
        pltpu.HBM if i in far else pltpu.SMEM if i in scalars else pltpu.VMEM for i in range(len(args))
    ]
    held = [pltpu.VMEM(*s) for s in scratch]
    if far:
        held.append(pltpu.SemaphoreType.DMA((5,)))
    if far_outs:
        held.append(pltpu.SemaphoreType.DMA((8,)))
    return pl.pallas_call(
        body,
        out_shape=[jax.ShapeDtypeStruct(s, d) for s, d in outs],
        in_specs=[pl.BlockSpec(memory_space=space) for space in spaces],
        out_specs=[
            pl.BlockSpec(memory_space=pltpu.HBM if i in far_outs else pltpu.VMEM)
            for i in range(len(outs))
        ],
        scratch_shapes=held,
        cost_estimate=pl.CostEstimate(flops=flops, bytes_accessed=size, transcendentals=0),
        compiler_params=pltpu.CompilerParams(vmem_limit_bytes=(58 if far else 12) << 20),
    )(*args)


def on_device(tokens, gates, experts, gate_weight, up_weight, down_weight, out_grad):
    AXIS["dp"] = lax.axis_size("dp")
    toks, width = tokens.shape
    hid = gate_weight.shape[2]
    count = lax.axis_size("expert") * gate_weight.shape[0]
    send = (count * 8, 3 * width // 2)
    slots = count * 12
    experts_t, gates_t = experts.T, gates.T

    def exchange(rows):
        moved = lax.all_to_all(
            rows.reshape(count, 8, send[1]),
            "expert",
            split_axis=0,
            concat_axis=0,
            tiled=True,
            axis_index_groups=[[y * 4 + x for x in range(4) for y in range(8)]],
        )
        return moved.reshape(send)

    pack_flops = 2 * send[0] * toks * send[1]
    (send_tok,) = call(pack_tokens, [(send, BF)], [], pack_flops, experts_t, tokens)
    shards, send_tok = lax.optimization_barrier(((gate_weight, up_weight, down_weight), send_tok))
    dp = lax.axis_size("dp")
    chips = dp // 2
    swap = [(i, i ^ 1) for i in range(dp)]

    def along(rows, steps):
        pairs = [(z * 2 + c, (z + steps) % chips * 2 + c) for z in range(chips) for c in range(2)]
        return lax.ppermute(rows, "dp", pairs)

    shard = jnp.concatenate(shards, axis=2)[0]
    mine = jnp.concatenate([shard] + [along(shard, k) for k in range(1, chips)], axis=0)
    other = lax.ppermute(mine, "dp", swap)
    (send_grad,) = call(pack_grads, [(send, BF)], [], pack_flops, experts_t, gates_t, out_grad)
    got_tok = exchange(send_tok)
    got_tok, send_grad = lax.optimization_barrier((got_tok, send_grad))
    got_grad = exchange(send_grad)
    index = lax.axis_index("dp")
    place = jnp.stack([index // 2, index % 2]).astype(jnp.int32)
    send_out, turned, gate_pre, up_pre = call(
        forward_rows,
        [(send, BF), ((slots, width), BF), ((slots, hid), F32), ((slots, hid), F32)],
        [((slots, hid), BF), ((slots - send[0], width), BF)],
        6 * slots * width * hid,
        place,
        got_tok,
        mine,
        other,
        scalars=(0,),
    )
    got_grad, send_out = lax.optimization_barrier((got_grad, send_out))
    got_out = exchange(send_out)
    half = (width // 2, 2 * hid)
    pre_grads, keep, give = call(
        backward_hidden,
        [((slots, 2 * hid), BF), (half, BF), (half, BF)],
        [
            ((slots, width), BF),
            ((width // 2, hid), BF),
            ((width // 2, hid), BF),
            ((slots, hid), F32),
            ((slots, hid), F32),
            ((slots, width), BF),
            ((width, 2 * hid), BF),
            ((slots - send[0], width), BF),
        ],
        6 * slots * width * hid,
        place,
        got_grad,
        mine,
        other,
        gate_pre,
        up_pre,
        turned,
        far=(2, 3, 4, 5, 6),
        far_outs=(1, 2),
        scalars=(0,),
    )
    taken = lax.ppermute(give, "dp", swap)
    pair = (keep.astype(F32) + taken.astype(F32)).astype(BF).reshape(chips, width // dp, 2 * hid)
    parts = {k: along(pair[k], -k) for k in range(1, chips) if k in EARLY}
    late = [pair[k] for k in range(1, chips) if k not in EARLY]
    (send_back,) = call(
        backward_rows,
        [(send, BF)],
        [((width, 2 * hid), BF), ((slots - send[0], width), BF)],
        4 * slots * width * hid,
        place,
        pre_grads,
        mine,
        other,
        far=(2, 3),
        scalars=(0,),
    )
    got_out, send_back, late = lax.optimization_barrier((got_out, send_back, late))
    for k in range(1, chips):
        if k not in EARLY:
            parts[k] = along(late.pop(0), -k)
    summed = pair[0].astype(F32)
    for k in range(1, chips):
        summed = summed + parts[k].astype(F32)
    summed = summed[None]
    got_back = exchange(send_back)
    mixed, gate_grad = call(
        combine_out,
        [((toks, width), BF), ((toks, 2), F32)],
        [],
        40000000 * toks * send[0] * width * 2,
        experts_t,
        gates_t,
        got_out,
        out_grad,
    )
    experts_t, summed = lax.optimization_barrier(
        (experts_t, (summed[:, :, :hid], summed[:, :, hid:]))
    )
    (token_grad,) = call(
        combine_grads, [((toks, width), BF)], [], 4 * toks * send[0] * width, experts_t, got_back
    )
    return (mixed, token_grad, gate_grad, *summed)


def solution(mesh):
    return jax.shard_map(
        on_device,
        mesh=mesh,
        in_specs=(
            P(("dp", "expert"), None),
            P(("dp", "expert"), None),
            P(("dp", "expert"), None),
            P("expert", "dp", None),
            P("expert", "dp", None),
            P("expert", "dp", None),
            P(("dp", "expert"), None),
        ),
        out_specs=(
            P(("dp", "expert"), None),
            P(("dp", "expert"), None),
            P(("dp", "expert"), None),
            P("expert", "dp", None),
            P("expert", "dp", None),
        ),
        check_vma=False,
    )
```

```python
import functools

import jax
import jax.numpy as jnp
from jax import lax
from jax.experimental import pallas as pl
from jax.experimental.pallas import tpu as pltpu
from jax.sharding import PartitionSpec as P

BF = jnp.bfloat16
F32 = jnp.float32
TILE = 512
AXIS = {}
EARLY = (3, 4, 5)


def iota(shape, axis):
    return lax.broadcasted_iota(jnp.int32, shape, axis)


def dot(left, right):
    return jnp.dot(left, right, preferred_element_type=F32)


def dot_cols(left, right):
    return lax.dot_general(left, right, (((1,), (1,)), ((), ())), preferred_element_type=F32)


def turn(expert):
    return (expert & 3) * 8 + (expert >> 2)


def pick_ranks(experts_ref, count):
    first, second = turn(experts_ref[0:1, :]), turn(experts_ref[1:2, :])
    toks = experts_ref.shape[1]
    names = iota((count, toks), 0)
    is_first, is_second = names == first, names == second
    either = jnp.where(is_first | is_second, 1.0, 0.0).astype(BF)
    earlier = jnp.where(iota((toks, toks), 0) < iota((toks, toks), 1), 1.0, 0.0).astype(BF)
    before = dot(either, earlier)
    ranks = [
        jnp.sum(jnp.where(mask, before, 0.0), axis=0, keepdims=True).astype(jnp.int32)
        for mask in (is_first, is_second)
    ]
    return ((first, ranks[0]), (second, ranks[1]))


def wide_row(expert, rank):
    return jnp.where(rank < 8, expert * 8 + rank, -1)


def half_row(expert, rank, half):
    return jnp.where(rank >= 8, expert * 8 + half * 4 + rank - 8, -1)


def as_column(row):
    toks = row.shape[1]
    eye = iota((toks, toks), 0) == iota((toks, toks), 1)
    return jnp.sum(jnp.where(eye, row, jnp.zeros_like(row)), axis=1, keepdims=True)


def send_masks(experts_ref, count):
    rows = count * 8
    toks = experts_ref.shape[1]
    row = iota((rows, toks), 0)
    out = []
    for expert, rank in pick_ranks(experts_ref, count):
        out.append(
            (
                row == wide_row(expert, rank),
                row == half_row(expert, rank, 0),
                row == half_row(expert, rank, 1),
            )
        )
    return out


def one_hot(*masks):
    both = masks[0]
    for mask in masks[1:]:
        both = both | mask
    return jnp.where(both, 1.0, 0.0).astype(BF)


def pack_tokens(experts_ref, rows_ref, out_ref):
    count = out_ref.shape[0] // 8
    width = rows_ref.shape[1]
    half = width // 2
    first, second = send_masks(experts_ref, count)
    wide = one_hot(first[0], second[0])
    halves = [one_hot(first[1 + h], second[1 + h]) for h in range(2)]
    for c in range(0, width, TILE):
        out_ref[:, c : c + TILE] = dot(wide, rows_ref[:, c : c + TILE]).astype(BF)
    for c in range(0, half, TILE):
        out_ref[:, width + c : width + c + TILE] = (
            dot(halves[0], rows_ref[:, c : c + TILE])
            + dot(halves[1], rows_ref[:, half + c : half + c + TILE])
        ).astype(BF)


def pack_grads(experts_ref, gates_ref, rows_ref, out_ref):
    count = out_ref.shape[0] // 8
    width = rows_ref.shape[1]
    half = width // 2
    first, second = send_masks(experts_ref, count)
    gate0, gate1 = gates_ref[0:1, :], gates_ref[1:2, :]

    def gate_of(mask0, mask1):
        return jnp.sum(
            jnp.where(mask0, gate0, 0.0) + jnp.where(mask1, gate1, 0.0), axis=1, keepdims=True
        )

    wide = one_hot(first[0], second[0])
    wide_gate = gate_of(first[0], second[0])
    halves = [one_hot(first[1 + h], second[1 + h]) for h in range(2)]
    half_gate = gate_of(first[1] | first[2], second[1] | second[2])
    for c in range(0, width, TILE):
        out_ref[:, c : c + TILE] = (wide_gate * dot(wide, rows_ref[:, c : c + TILE])).astype(BF)
    for c in range(0, half, TILE):
        out_ref[:, width + c : width + c + TILE] = (
            half_gate
            * (
                dot(halves[0], rows_ref[:, c : c + TILE])
                + dot(halves[1], rows_ref[:, half + c : half + c + TILE])
            )
        ).astype(BF)


def fetch_masks(experts_ref, count):
    rows = count * 8
    toks = experts_ref.shape[1]
    col = iota((toks, rows), 1)
    out = []
    for expert, rank in pick_ranks(experts_ref, count):
        targets = (wide_row(expert, rank), half_row(expert, rank, 0), half_row(expert, rank, 1))
        out.append(tuple(col == as_column(t) for t in targets))
    return out


def combine_out(experts_ref, gates_ref, got_ref, grad_ref, mixed_ref, gate_grad_ref):
    count = got_ref.shape[0] // 8
    toks, width = mixed_ref.shape
    half = width // 2
    masks = fetch_masks(experts_ref, count)
    wide = [one_hot(m[0]) for m in masks]
    halves = [[one_hot(m[1 + h]) for m in masks] for h in range(2)]
    gates = [as_column(gates_ref[k : k + 1, :]) for k in range(2)]
    sums = [jnp.zeros((toks, 1), F32) for _ in range(2)]
    for c in range(0, width, TILE):
        h, low = c // half, width + c % half
        grad = grad_ref[:, c : c + TILE].astype(F32)
        total = jnp.zeros((toks, TILE), F32)
        for k in range(2):
            picked = dot(wide[k], got_ref[:, c : c + TILE]) + dot(
                halves[h][k], got_ref[:, low : low + TILE]
            )
            total = total + gates[k] * picked
            sums[k] = sums[k] + jnp.sum(grad * picked, axis=1, keepdims=True)
        mixed_ref[:, c : c + TILE] = total.astype(BF)
    lane = iota((toks, 2), 1)
    gate_grad_ref[...] = jnp.where(lane == 0, sums[0], sums[1])


def combine_grads(experts_ref, got_ref, out_ref):
    count = got_ref.shape[0] // 8
    width = out_ref.shape[1]
    half = width // 2
    first, second = fetch_masks(experts_ref, count)
    wide = one_hot(first[0], second[0])
    halves = [one_hot(first[1 + h], second[1 + h]) for h in range(2)]
    for c in range(0, width, TILE):
        low = width + c % half
        out_ref[:, c : c + TILE] = (
            dot(wide, got_ref[:, c : c + TILE]) + dot(halves[c // half], got_ref[:, low : low + TILE])
        ).astype(BF)


def turned_blocks(place_ref, width, size):
    z, core = place_ref[0], place_ref[1]
    chips = AXIS["dp"] // 2
    block = width // (2 * chips)
    size = min(size, block)
    pairs = []
    for side, owner in enumerate((core, 1 - core)):
        for k in range(chips):
            shard = 2 * lax.rem(z + (chips - k), chips) + owner
            for c in range(0, block, size):
                column = pl.multiple_of(shard * block + c, 128)
                pairs.append((side * (width // 2) + k * block + c, column))
    return size, pairs


def split_rows(place_ref, got_ref, rows_ref, tail_ref):
    count = got_ref.shape[0]
    width = rows_ref.shape[1]
    half = width // 2
    tail = count // 2
    row, col = iota((tail, count), 0), iota((tail, count), 1)
    for h in range(2):
        pick = one_hot(col == (row >> 2) * 8 + h * 4 + (row & 3))
        for c in range(0, half, TILE):
            tail_ref[:, h * half + c : h * half + c + TILE] = dot(
                pick, got_ref[:, width + c : width + c + TILE]
            ).astype(BF)
    size, pairs = turned_blocks(place_ref, width, TILE)
    for to, column in pairs:
        rows_ref[0:count, to : to + size] = got_ref[:, pl.ds(column, size)]
        rows_ref[count:, to : to + size] = tail_ref[:, pl.ds(column, size)]


def tail_spread(count):
    tail = count // 2
    row, col = iota((count, tail), 0), iota((count, tail), 1)
    return [one_hot(row == (col >> 2) * 8 + h * 4 + (col & 3)) for h in range(2)]


def store_rows(place_ref, product, send_ref, tail_ref, width, at):
    count = send_ref.shape[0]
    size, pairs = turned_blocks(place_ref, width, 256)
    for to, column in pairs:
        if at <= to < at + 256:
            send_ref[:, pl.ds(column, size)] = product[0:count, to - at : to - at + size]
            tail_ref[:, pl.ds(column, size)] = product[count:, to - at : to - at + size]


def flush_tail(send_ref, tail_ref, width):
    count = send_ref.shape[0]
    half = width // 2
    spread = tail_spread(count)
    for c in range(0, half, TILE):
        send_ref[:, width + c : width + c + TILE] = (
            dot(spread[0], tail_ref[:, c : c + TILE])
            + dot(spread[1], tail_ref[:, half + c : half + c + TILE])
        ).astype(BF)


def dot_turned(rows_ref, mine_ref, other_ref, columns):
    half = mine_ref.shape[0]
    return dot(rows_ref[:, 0:half], mine_ref[:, columns]) + dot(
        rows_ref[:, half:], other_ref[:, columns]
    )


def forward_rows(
    place_ref, got_ref, mine_ref, other_ref, send_ref, rows_ref, gate_ref, up_ref, hidden_ref, tail_ref
):
    width = rows_ref.shape[1]
    half = width // 2
    hid = gate_ref.shape[1]
    split_rows(place_ref, got_ref, rows_ref, tail_ref)
    for c in range(0, hid, 256):
        gate = dot_turned(rows_ref, mine_ref, other_ref, slice(c, c + 256))
        up = dot_turned(rows_ref, mine_ref, other_ref, slice(hid + c, hid + c + 256))
        gate_ref[:, c : c + 256] = gate
        up_ref[:, c : c + 256] = up
        hidden_ref[:, c : c + 256] = (gate * jax.nn.sigmoid(gate) * up).astype(BF)
    for side, weights_ref in enumerate((mine_ref, other_ref)):
        for c in range(0, half, 256):
            product = dot_cols(hidden_ref[...], weights_ref[c : c + 256, 2 * hid : 3 * hid])
            store_rows(place_ref, product.astype(BF), send_ref, tail_ref, width, side * half + c)
    flush_tail(send_ref, tail_ref, width)


def backward_hidden(
    place_ref, got_ref, mine_ref, other_ref, gate_ref, up_ref, turned_ref,
    pre_ref, keep_ref, give_ref,
    rows_ref, mine_in, other_in, gate_in, up_in, turned_in, sums_ref, tail_ref, sems, out_sems,
):
    width = rows_ref.shape[1]
    hid = gate_ref.shape[1]
    copies = [
        pltpu.make_async_copy(source, target, sems.at[i])
        for i, (source, target) in enumerate(
            (
                (mine_ref.at[:, pl.ds(2 * hid, hid)], mine_in),
                (other_ref.at[:, pl.ds(2 * hid, hid)], other_in),
                (gate_ref, gate_in),
                (up_ref, up_in),
                (turned_ref, turned_in),
            )
        )
    ]
    for copy in copies:
        copy.start()
    split_rows(place_ref, got_ref, rows_ref, tail_ref)
    for copy in copies[:4]:
        copy.wait()
    for c in range(0, hid, 256):
        grad = dot_turned(rows_ref, mine_in, other_in, slice(c, c + 256))
        gate, up = gate_in[:, c : c + 256], up_in[:, c : c + 256]
        sigma = jax.nn.sigmoid(gate)
        pre_ref[:, hid + c : hid + c + 256] = (grad * gate * sigma).astype(BF)
        pre_ref[:, c : c + 256] = (grad * up * sigma * (1.0 + gate * (1.0 - sigma))).astype(BF)
    copies[4].wait()
    leaving = []
    for side, out_ref in ((1, give_ref), (0, keep_ref)):
        for c in range(0, width // 2, 256):
            at = side * (width // 2) + c
            sums_ref[at : at + 256, :] = lax.dot_general(
                turned_in[:, at : at + 256],
                pre_ref[...],
                (((0,), (0,)), ((), ())),
                preferred_element_type=F32,
            ).astype(BF)
            leaving.append(
                pltpu.make_async_copy(
                    sums_ref.at[pl.ds(at, 256)], out_ref.at[pl.ds(c, 256)], out_sems.at[at // 256]
                )
            )
            leaving[-1].start()
    for copy in leaving:
        copy.wait()


def backward_rows(place_ref, pre_ref, mine_ref, other_ref, send_ref, both_in, tail_ref, sems):
    half = mine_ref.shape[0]
    both = pre_ref.shape[1]
    size = half // 2
    copies = []
    for i in range(4):
        source = (mine_ref, other_ref)[i // 2]
        copies.append(
            pltpu.make_async_copy(
                source.at[pl.ds(i % 2 * size, size), pl.ds(0, both)],
                both_in.at[pl.ds(i * size, size)],
                sems.at[i],
            )
        )
        copies[-1].start()
    for i in range(4):
        copies[i].wait()
        for c in range(i * size, (i + 1) * size, 256):
            product = dot_cols(pre_ref[...], both_in[c : c + 256, :]).astype(BF)
            store_rows(place_ref, product, send_ref, tail_ref, 2 * half, c)
    flush_tail(send_ref, tail_ref, 2 * half)


def call(body, outs, scratch, flops, *args, far=(), far_outs=(), scalars=()):
    size = sum(a.size * a.dtype.itemsize for a in args)
    size += sum(o[0][0] * o[0][1] * jnp.dtype(o[1]).itemsize for o in outs)
    spaces = [
        pltpu.HBM if i in far else pltpu.SMEM if i in scalars else pltpu.VMEM for i in range(len(args))
    ]
    held = [pltpu.VMEM(*s) for s in scratch]
    if far:
        held.append(pltpu.SemaphoreType.DMA((5,)))
    if far_outs:
        held.append(pltpu.SemaphoreType.DMA((8,)))
    return pl.pallas_call(
        body,
        out_shape=[jax.ShapeDtypeStruct(s, d) for s, d in outs],
        in_specs=[pl.BlockSpec(memory_space=space) for space in spaces],
        out_specs=[
            pl.BlockSpec(memory_space=pltpu.HBM if i in far_outs else pltpu.VMEM)
            for i in range(len(outs))
        ],
        scratch_shapes=held,
        cost_estimate=pl.CostEstimate(flops=flops, bytes_accessed=size, transcendentals=0),
        compiler_params=pltpu.CompilerParams(vmem_limit_bytes=(58 if far else 12) << 20),
    )(*args)


def on_device(tokens, gates, experts, gate_weight, up_weight, down_weight, out_grad):
    AXIS["dp"] = lax.axis_size("dp")
    toks, width = tokens.shape
    hid = gate_weight.shape[2]
    count = lax.axis_size("expert") * gate_weight.shape[0]
    send = (count * 8, 3 * width // 2)
    slots = count * 12
    experts_t, gates_t = experts.T, gates.T

    def exchange(rows):
        moved = lax.all_to_all(
            rows.reshape(count, 8, send[1]),
            "expert",
            split_axis=0,
            concat_axis=0,
            tiled=True,
            axis_index_groups=[[y * 4 + x for x in range(4) for y in range(8)]],
        )
        return moved.reshape(send)

    pack_flops = 2 * send[0] * toks * send[1]
    (send_tok,) = call(pack_tokens, [(send, BF)], [], pack_flops, experts_t, tokens)
    shards, send_tok = lax.optimization_barrier(((gate_weight, up_weight, down_weight), send_tok))
    dp = lax.axis_size("dp")
    chips = dp // 2
    swap = [(i, i ^ 1) for i in range(dp)]

    def along(rows, steps):
        pairs = [(z * 2 + c, (z + steps) % chips * 2 + c) for z in range(chips) for c in range(2)]
        return lax.ppermute(rows, "dp", pairs)

    shard = jnp.concatenate(shards, axis=2)[0]
    came = {0: shard}
    for k in range(1, chips // 2 + 1):
        came[k] = along(came[k - 1], 1)
    for k in range(chips - 1, chips // 2, -1):
        came[k] = along(came[(k + 1) % chips], -1)
    mine = jnp.concatenate([came[k] for k in range(chips)], axis=0)
    other = lax.ppermute(mine, "dp", swap)
    (send_grad,) = call(pack_grads, [(send, BF)], [], pack_flops, experts_t, gates_t, out_grad)
    got_tok = exchange(send_tok)
    got_tok, send_grad = lax.optimization_barrier((got_tok, send_grad))
    got_grad = exchange(send_grad)
    index = lax.axis_index("dp")
    place = jnp.stack([index // 2, index % 2]).astype(jnp.int32)
    send_out, turned, gate_pre, up_pre = call(
        forward_rows,
        [(send, BF), ((slots, width), BF), ((slots, hid), F32), ((slots, hid), F32)],
        [((slots, hid), BF), ((slots - send[0], width), BF)],
        6 * slots * width * hid,
        place,
        got_tok,
        mine,
        other,
        scalars=(0,),
    )
    got_grad, send_out = lax.optimization_barrier((got_grad, send_out))
    got_out = exchange(send_out)
    half = (width // 2, 2 * hid)
    pre_grads, keep, give = call(
        backward_hidden,
        [((slots, 2 * hid), BF), (half, BF), (half, BF)],
        [
            ((slots, width), BF),
            ((width // 2, hid), BF),
            ((width // 2, hid), BF),
            ((slots, hid), F32),
            ((slots, hid), F32),
            ((slots, width), BF),
            ((width, 2 * hid), BF),
            ((slots - send[0], width), BF),
        ],
        6 * slots * width * hid,
        place,
        got_grad,
        mine,
        other,
        gate_pre,
        up_pre,
        turned,
        far=(2, 3, 4, 5, 6),
        far_outs=(1, 2),
        scalars=(0,),
    )
    taken = lax.ppermute(give, "dp", swap)
    pair = (keep.astype(F32) + taken.astype(F32)).astype(BF).reshape(chips, width // dp, 2 * hid)
    parts = {k: along(pair[k], -k) for k in range(1, chips) if k in EARLY}
    late = [pair[k] for k in range(1, chips) if k not in EARLY]
    (send_back,) = call(
        backward_rows,
        [(send, BF)],
        [((width, 2 * hid), BF), ((slots - send[0], width), BF)],
        4 * slots * width * hid,
        place,
        pre_grads,
        mine,
        other,
        far=(2, 3),
        scalars=(0,),
    )
    got_out, send_back, late = lax.optimization_barrier((got_out, send_back, late))
    for k in range(1, chips):
        if k not in EARLY:
            parts[k] = along(late.pop(0), -k)
    summed = pair[0].astype(F32)
    for k in range(1, chips):
        summed = summed + parts[k].astype(F32)
    summed = summed[None]
    got_back = exchange(send_back)
    mixed, gate_grad = call(
        combine_out,
        [((toks, width), BF), ((toks, 2), F32)],
        [],
        40000000 * toks * send[0] * width * 2,
        experts_t,
        gates_t,
        got_out,
        out_grad,
    )
    experts_t, summed = lax.optimization_barrier(
        (experts_t, (summed[:, :, :hid], summed[:, :, hid:]))
    )
    (token_grad,) = call(
        combine_grads, [((toks, width), BF)], [], 4 * toks * send[0] * width, experts_t, got_back
    )
    return (mixed, token_grad, gate_grad, *summed)


def solution(mesh):
    return jax.shard_map(
        on_device,
        mesh=mesh,
        in_specs=(
            P(("dp", "expert"), None),
            P(("dp", "expert"), None),
            P(("dp", "expert"), None),
            P("expert", "dp", None),
            P("expert", "dp", None),
            P("expert", "dp", None),
            P(("dp", "expert"), None),
        ),
        out_specs=(
            P(("dp", "expert"), None),
            P(("dp", "expert"), None),
            P(("dp", "expert"), None),
            P("expert", "dp", None),
            P("expert", "dp", None),
        ),
        check_vma=False,
    )
```

```python
import functools

import jax
import jax.numpy as jnp
from jax import lax
from jax.experimental import pallas as pl
from jax.experimental.pallas import tpu as pltpu
from jax.sharding import PartitionSpec as P

BF = jnp.bfloat16
F32 = jnp.float32
TILE = 512
AXIS = {}
EARLY = (3, 4, 5)


def iota(shape, axis):
    return lax.broadcasted_iota(jnp.int32, shape, axis)


def dot(left, right):
    return jnp.dot(left, right, preferred_element_type=F32)


def dot_cols(left, right):
    return lax.dot_general(left, right, (((1,), (1,)), ((), ())), preferred_element_type=F32)


def turn(expert):
    return (expert & 3) * 8 + (expert >> 2)


def pick_ranks(experts_ref, count):
    first, second = turn(experts_ref[0:1, :]), turn(experts_ref[1:2, :])
    toks = experts_ref.shape[1]
    names = iota((count, toks), 0)
    is_first, is_second = names == first, names == second
    either = jnp.where(is_first | is_second, 1.0, 0.0).astype(BF)
    earlier = jnp.where(iota((toks, toks), 0) < iota((toks, toks), 1), 1.0, 0.0).astype(BF)
    before = dot(either, earlier)
    ranks = [
        jnp.sum(jnp.where(mask, before, 0.0), axis=0, keepdims=True).astype(jnp.int32)
        for mask in (is_first, is_second)
    ]
    return ((first, ranks[0]), (second, ranks[1]))


def wide_row(expert, rank):
    return jnp.where(rank < 8, expert * 8 + rank, -1)


def half_row(expert, rank, half):
    return jnp.where(rank >= 8, expert * 8 + half * 4 + rank - 8, -1)


def as_column(row):
    toks = row.shape[1]
    eye = iota((toks, toks), 0) == iota((toks, toks), 1)
    return jnp.sum(jnp.where(eye, row, jnp.zeros_like(row)), axis=1, keepdims=True)


def send_masks(experts_ref, count):
    rows = count * 8
    toks = experts_ref.shape[1]
    row = iota((rows, toks), 0)
    out = []
    for expert, rank in pick_ranks(experts_ref, count):
        out.append(
            (
                row == wide_row(expert, rank),
                row == half_row(expert, rank, 0),
                row == half_row(expert, rank, 1),
            )
        )
    return out


def one_hot(*masks):
    both = masks[0]
    for mask in masks[1:]:
        both = both | mask
    return jnp.where(both, 1.0, 0.0).astype(BF)


def pack_tokens(experts_ref, rows_ref, out_ref):
    count = out_ref.shape[0] // 8
    width = rows_ref.shape[1]
    half = width // 2
    first, second = send_masks(experts_ref, count)
    wide = one_hot(first[0], second[0])
    halves = [one_hot(first[1 + h], second[1 + h]) for h in range(2)]
    for c in range(0, width, TILE):
        out_ref[:, c : c + TILE] = dot(wide, rows_ref[:, c : c + TILE]).astype(BF)
    for c in range(0, half, TILE):
        out_ref[:, width + c : width + c + TILE] = (
            dot(halves[0], rows_ref[:, c : c + TILE])
            + dot(halves[1], rows_ref[:, half + c : half + c + TILE])
        ).astype(BF)


def pack_grads(experts_ref, gates_ref, rows_ref, out_ref):
    count = out_ref.shape[0] // 8
    width = rows_ref.shape[1]
    half = width // 2
    first, second = send_masks(experts_ref, count)
    gate0, gate1 = gates_ref[0:1, :], gates_ref[1:2, :]

    def gate_of(mask0, mask1):
        return jnp.sum(
            jnp.where(mask0, gate0, 0.0) + jnp.where(mask1, gate1, 0.0), axis=1, keepdims=True
        )

    wide = one_hot(first[0], second[0])
    wide_gate = gate_of(first[0], second[0])
    halves = [one_hot(first[1 + h], second[1 + h]) for h in range(2)]
    half_gate = gate_of(first[1] | first[2], second[1] | second[2])
    for c in range(0, width, TILE):
        out_ref[:, c : c + TILE] = (wide_gate * dot(wide, rows_ref[:, c : c + TILE])).astype(BF)
    for c in range(0, half, TILE):
        out_ref[:, width + c : width + c + TILE] = (
            half_gate
            * (
                dot(halves[0], rows_ref[:, c : c + TILE])
                + dot(halves[1], rows_ref[:, half + c : half + c + TILE])
            )
        ).astype(BF)


def fetch_masks(experts_ref, count):
    rows = count * 8
    toks = experts_ref.shape[1]
    col = iota((toks, rows), 1)
    out = []
    for expert, rank in pick_ranks(experts_ref, count):
        targets = (wide_row(expert, rank), half_row(expert, rank, 0), half_row(expert, rank, 1))
        out.append(tuple(col == as_column(t) for t in targets))
    return out


def combine_out(experts_ref, gates_ref, got_ref, grad_ref, mixed_ref, gate_grad_ref):
    count = got_ref.shape[0] // 8
    toks, width = mixed_ref.shape
    half = width // 2
    masks = fetch_masks(experts_ref, count)
    wide = [one_hot(m[0]) for m in masks]
    halves = [[one_hot(m[1 + h]) for m in masks] for h in range(2)]
    gates = [as_column(gates_ref[k : k + 1, :]) for k in range(2)]
    sums = [jnp.zeros((toks, 1), F32) for _ in range(2)]
    for c in range(0, width, TILE):
        h, low = c // half, width + c % half
        grad = grad_ref[:, c : c + TILE].astype(F32)
        total = jnp.zeros((toks, TILE), F32)
        for k in range(2):
            picked = dot(wide[k], got_ref[:, c : c + TILE]) + dot(
                halves[h][k], got_ref[:, low : low + TILE]
            )
            total = total + gates[k] * picked
            sums[k] = sums[k] + jnp.sum(grad * picked, axis=1, keepdims=True)
        mixed_ref[:, c : c + TILE] = total.astype(BF)
    lane = iota((toks, 2), 1)
    gate_grad_ref[...] = jnp.where(lane == 0, sums[0], sums[1])


def combine_grads(experts_ref, got_ref, out_ref):
    count = got_ref.shape[0] // 8
    width = out_ref.shape[1]
    half = width // 2
    first, second = fetch_masks(experts_ref, count)
    wide = one_hot(first[0], second[0])
    halves = [one_hot(first[1 + h], second[1 + h]) for h in range(2)]
    for c in range(0, width, TILE):
        low = width + c % half
        out_ref[:, c : c + TILE] = (
            dot(wide, got_ref[:, c : c + TILE]) + dot(halves[c // half], got_ref[:, low : low + TILE])
        ).astype(BF)


def turned_blocks(place_ref, width, size):
    z, core = place_ref[0], place_ref[1]
    chips = AXIS["dp"] // 2
    block = width // (2 * chips)
    size = min(size, block)
    pairs = []
    for side, owner in enumerate((core, 1 - core)):
        for k in range(chips):
            shard = 2 * lax.rem(z + (chips - k), chips) + owner
            for c in range(0, block, size):
                column = pl.multiple_of(shard * block + c, 128)
                pairs.append((side * (width // 2) + k * block + c, column))
    return size, pairs


def split_rows(place_ref, got_ref, rows_ref, tail_ref):
    count = got_ref.shape[0]
    width = rows_ref.shape[1]
    half = width // 2
    tail = count // 2
    row, col = iota((tail, count), 0), iota((tail, count), 1)
    for h in range(2):
        pick = one_hot(col == (row >> 2) * 8 + h * 4 + (row & 3))
        for c in range(0, half, TILE):
            tail_ref[:, h * half + c : h * half + c + TILE] = dot(
                pick, got_ref[:, width + c : width + c + TILE]
            ).astype(BF)
    size, pairs = turned_blocks(place_ref, width, TILE)
    for to, column in pairs:
        rows_ref[0:count, to : to + size] = got_ref[:, pl.ds(column, size)]
        rows_ref[count:, to : to + size] = tail_ref[:, pl.ds(column, size)]


def tail_spread(count):
    tail = count // 2
    row, col = iota((count, tail), 0), iota((count, tail), 1)
    return [one_hot(row == (col >> 2) * 8 + h * 4 + (col & 3)) for h in range(2)]


def store_rows(place_ref, product, send_ref, tail_ref, width, at):
    count = send_ref.shape[0]
    size, pairs = turned_blocks(place_ref, width, 256)
    for to, column in pairs:
        if at <= to < at + 256:
            send_ref[:, pl.ds(column, size)] = product[0:count, to - at : to - at + size]
            tail_ref[:, pl.ds(column, size)] = product[count:, to - at : to - at + size]


def flush_tail(send_ref, tail_ref, width):
    count = send_ref.shape[0]
    half = width // 2
    spread = tail_spread(count)
    for c in range(0, half, TILE):
        send_ref[:, width + c : width + c + TILE] = (
            dot(spread[0], tail_ref[:, c : c + TILE])
            + dot(spread[1], tail_ref[:, half + c : half + c + TILE])
        ).astype(BF)


def dot_turned(rows_ref, mine_ref, other_ref, columns):
    half = mine_ref.shape[0]
    return dot(rows_ref[:, 0:half], mine_ref[:, columns]) + dot(
        rows_ref[:, half:], other_ref[:, columns]
    )


def forward_rows(
    place_ref, got_ref, mine_ref, other_ref, send_ref, rows_ref, gate_ref, up_ref, hidden_ref, tail_ref
):
    width = rows_ref.shape[1]
    half = width // 2
    hid = gate_ref.shape[1]
    split_rows(place_ref, got_ref, rows_ref, tail_ref)
    for c in range(0, hid, 256):
        gate = dot_turned(rows_ref, mine_ref, other_ref, slice(c, c + 256))
        up = dot_turned(rows_ref, mine_ref, other_ref, slice(hid + c, hid + c + 256))
        gate_ref[:, c : c + 256] = gate
        up_ref[:, c : c + 256] = up
        hidden_ref[:, c : c + 256] = (gate * jax.nn.sigmoid(gate) * up).astype(BF)
    for side, weights_ref in enumerate((mine_ref, other_ref)):
        for c in range(0, half, 256):
            product = dot_cols(hidden_ref[...], weights_ref[c : c + 256, 2 * hid : 3 * hid])
            store_rows(place_ref, product.astype(BF), send_ref, tail_ref, width, side * half + c)
    flush_tail(send_ref, tail_ref, width)


def backward_hidden(
    place_ref, got_ref, mine_ref, other_ref, gate_ref, up_ref, turned_ref,
    pre_ref, keep_ref, give_ref,
    rows_ref, mine_in, other_in, gate_in, up_in, turned_in, sums_ref, tail_ref, sems, out_sems,
):
    width = rows_ref.shape[1]
    hid = gate_ref.shape[1]
    copies = [
        pltpu.make_async_copy(source, target, sems.at[i])
        for i, (source, target) in enumerate(
            (
                (mine_ref.at[:, pl.ds(2 * hid, hid)], mine_in),
                (other_ref.at[:, pl.ds(2 * hid, hid)], other_in),
                (gate_ref, gate_in),
                (up_ref, up_in),
                (turned_ref, turned_in),
            )
        )
    ]
    for copy in copies:
        copy.start()
    split_rows(place_ref, got_ref, rows_ref, tail_ref)
    for copy in copies[:4]:
        copy.wait()
    for c in range(0, hid, 256):
        grad = dot_turned(rows_ref, mine_in, other_in, slice(c, c + 256))
        gate, up = gate_in[:, c : c + 256], up_in[:, c : c + 256]
        sigma = jax.nn.sigmoid(gate)
        pre_ref[:, hid + c : hid + c + 256] = (grad * gate * sigma).astype(BF)
        pre_ref[:, c : c + 256] = (grad * up * sigma * (1.0 + gate * (1.0 - sigma))).astype(BF)
    copies[4].wait()
    leaving = []
    for side, out_ref in ((1, give_ref), (0, keep_ref)):
        for c in range(0, width // 2, 256):
            at = side * (width // 2) + c
            sums_ref[at : at + 256, :] = lax.dot_general(
                turned_in[:, at : at + 256],
                pre_ref[...],
                (((0,), (0,)), ((), ())),
                preferred_element_type=F32,
            ).astype(BF)
            leaving.append(
                pltpu.make_async_copy(
                    sums_ref.at[pl.ds(at, 256)], out_ref.at[pl.ds(c, 256)], out_sems.at[at // 256]
                )
            )
            leaving[-1].start()
    for copy in leaving:
        copy.wait()


def backward_rows(place_ref, pre_ref, mine_ref, other_ref, send_ref, both_in, tail_ref, sems):
    half = mine_ref.shape[0]
    both = pre_ref.shape[1]
    size = half // 2
    copies = []
    for i in range(4):
        source = (mine_ref, other_ref)[i // 2]
        copies.append(
            pltpu.make_async_copy(
                source.at[pl.ds(i % 2 * size, size), pl.ds(0, both)],
                both_in.at[pl.ds(i * size, size)],
                sems.at[i],
            )
        )
        copies[-1].start()
    for i in range(4):
        copies[i].wait()
        for c in range(i * size, (i + 1) * size, 256):
            product = dot_cols(pre_ref[...], both_in[c : c + 256, :]).astype(BF)
            store_rows(place_ref, product, send_ref, tail_ref, 2 * half, c)
    flush_tail(send_ref, tail_ref, 2 * half)


def call(body, outs, scratch, flops, *args, far=(), far_outs=(), scalars=()):
    size = sum(a.size * a.dtype.itemsize for a in args)
    size += sum(o[0][0] * o[0][1] * jnp.dtype(o[1]).itemsize for o in outs)
    spaces = [
        pltpu.HBM if i in far else pltpu.SMEM if i in scalars else pltpu.VMEM for i in range(len(args))
    ]
    held = [pltpu.VMEM(*s) for s in scratch]
    if far:
        held.append(pltpu.SemaphoreType.DMA((5,)))
    if far_outs:
        held.append(pltpu.SemaphoreType.DMA((8,)))
    return pl.pallas_call(
        body,
        out_shape=[jax.ShapeDtypeStruct(s, d) for s, d in outs],
        in_specs=[pl.BlockSpec(memory_space=space) for space in spaces],
        out_specs=[
            pl.BlockSpec(memory_space=pltpu.HBM if i in far_outs else pltpu.VMEM)
            for i in range(len(outs))
        ],
        scratch_shapes=held,
        cost_estimate=pl.CostEstimate(flops=flops, bytes_accessed=size, transcendentals=0),
        compiler_params=pltpu.CompilerParams(vmem_limit_bytes=(58 if far else 12) << 20),
    )(*args)


def on_device(tokens, gates, experts, gate_weight, up_weight, down_weight, out_grad):
    AXIS["dp"] = lax.axis_size("dp")
    toks, width = tokens.shape
    hid = gate_weight.shape[2]
    count = lax.axis_size("expert") * gate_weight.shape[0]
    send = (count * 8, 3 * width // 2)
    slots = count * 12
    experts_t, gates_t = experts.T, gates.T

    def exchange(rows):
        moved = lax.all_to_all(
            rows.reshape(count, 8, send[1]),
            "expert",
            split_axis=0,
            concat_axis=0,
            tiled=True,
            axis_index_groups=[[y * 4 + x for x in range(4) for y in range(8)]],
        )
        return moved.reshape(send)

    pack_flops = 2 * send[0] * toks * send[1]
    (send_tok,) = call(pack_tokens, [(send, BF)], [], pack_flops, experts_t, tokens)
    shards, send_tok = lax.optimization_barrier(((gate_weight, up_weight, down_weight), send_tok))
    dp = lax.axis_size("dp")
    chips = dp // 2
    swap = [(i, i ^ 1) for i in range(dp)]

    def along(rows, steps):
        pairs = [(z * 2 + c, (z + steps) % chips * 2 + c) for z in range(chips) for c in range(2)]
        return lax.ppermute(rows, "dp", pairs)

    shard = jnp.concatenate(shards, axis=2)[0]
    came = {0: shard}
    for k in range(1, chips // 2 + 1):
        came[k] = along(came[k - 1], 1)
    for k in range(chips - 1, chips // 2, -1):
        came[k] = along(came[(k + 1) % chips], -1)
    mine = jnp.concatenate([came[k] for k in range(chips)], axis=0)
    other = jnp.concatenate([lax.ppermute(came[k], "dp", swap) for k in range(chips)], axis=0)
    (send_grad,) = call(pack_grads, [(send, BF)], [], pack_flops, experts_t, gates_t, out_grad)
    got_tok = exchange(send_tok)
    got_tok, send_grad = lax.optimization_barrier((got_tok, send_grad))
    got_grad = exchange(send_grad)
    index = lax.axis_index("dp")
    place = jnp.stack([index // 2, index % 2]).astype(jnp.int32)
    send_out, turned, gate_pre, up_pre = call(
        forward_rows,
        [(send, BF), ((slots, width), BF), ((slots, hid), F32), ((slots, hid), F32)],
        [((slots, hid), BF), ((slots - send[0], width), BF)],
        6 * slots * width * hid,
        place,
        got_tok,
        mine,
        other,
        scalars=(0,),
    )
    got_grad, send_out = lax.optimization_barrier((got_grad, send_out))
    got_out = exchange(send_out)
    half = (width // 2, 2 * hid)
    pre_grads, keep, give = call(
        backward_hidden,
        [((slots, 2 * hid), BF), (half, BF), (half, BF)],
        [
            ((slots, width), BF),
            ((width // 2, hid), BF),
            ((width // 2, hid), BF),
            ((slots, hid), F32),
            ((slots, hid), F32),
            ((slots, width), BF),
            ((width, 2 * hid), BF),
            ((slots - send[0], width), BF),
        ],
        6 * slots * width * hid,
        place,
        got_grad,
        mine,
        other,
        gate_pre,
        up_pre,
        turned,
        far=(2, 3, 4, 5, 6),
        far_outs=(1, 2),
        scalars=(0,),
    )
    taken = lax.ppermute(give, "dp", swap)
    pair = (keep.astype(F32) + taken.astype(F32)).astype(BF).reshape(chips, width // dp, 2 * hid)
    parts = {k: along(pair[k], -k) for k in range(1, chips) if k in EARLY}
    late = [pair[k] for k in range(1, chips) if k not in EARLY]
    (send_back,) = call(
        backward_rows,
        [(send, BF)],
        [((width, 2 * hid), BF), ((slots - send[0], width), BF)],
        4 * slots * width * hid,
        place,
        pre_grads,
        mine,
        other,
        far=(2, 3),
        scalars=(0,),
    )
    got_out, send_back, late = lax.optimization_barrier((got_out, send_back, late))
    for k in range(1, chips):
        if k not in EARLY:
            parts[k] = along(late.pop(0), -k)
    summed = pair[0].astype(F32)
    for k in range(1, chips):
        summed = summed + parts[k].astype(F32)
    summed = summed[None]
    got_back = exchange(send_back)
    mixed, gate_grad = call(
        combine_out,
        [((toks, width), BF), ((toks, 2), F32)],
        [],
        40000000 * toks * send[0] * width * 2,
        experts_t,
        gates_t,
        got_out,
        out_grad,
    )
    experts_t, summed = lax.optimization_barrier(
        (experts_t, (summed[:, :, :hid], summed[:, :, hid:]))
    )
    (token_grad,) = call(
        combine_grads, [((toks, width), BF)], [], 4 * toks * send[0] * width, experts_t, got_back
    )
    return (mixed, token_grad, gate_grad, *summed)


def solution(mesh):
    return jax.shard_map(
        on_device,
        mesh=mesh,
        in_specs=(
            P(("dp", "expert"), None),
            P(("dp", "expert"), None),
            P(("dp", "expert"), None),
            P("expert", "dp", None),
            P("expert", "dp", None),
            P("expert", "dp", None),
            P(("dp", "expert"), None),
        ),
        out_specs=(
            P(("dp", "expert"), None),
            P(("dp", "expert"), None),
            P(("dp", "expert"), None),
            P("expert", "dp", None),
            P("expert", "dp", None),
        ),
        check_vma=False,
    )
```

```python
import functools

import jax
import jax.numpy as jnp
from jax import lax
from jax.experimental import pallas as pl
from jax.experimental.pallas import tpu as pltpu
from jax.sharding import PartitionSpec as P

BF = jnp.bfloat16
F32 = jnp.float32
TILE = 512


def iota(shape, axis):
    return lax.broadcasted_iota(jnp.int32, shape, axis)


def dot(left, right):
    return jnp.dot(left, right, preferred_element_type=F32)


def dot_cols(left, right):
    return lax.dot_general(left, right, (((1,), (1,)), ((), ())), preferred_element_type=F32)


def turn(expert):
    return (expert & 3) * 8 + (expert >> 2)


def pick_ranks(experts_ref, count):
    first, second = turn(experts_ref[0:1, :]), turn(experts_ref[1:2, :])
    toks = experts_ref.shape[1]
    names = iota((count, toks), 0)
    is_first, is_second = names == first, names == second
    either = jnp.where(is_first | is_second, 1.0, 0.0).astype(BF)
    earlier = jnp.where(iota((toks, toks), 0) < iota((toks, toks), 1), 1.0, 0.0).astype(BF)
    before = dot(either, earlier)
    ranks = [
        jnp.sum(jnp.where(mask, before, 0.0), axis=0, keepdims=True).astype(jnp.int32)
        for mask in (is_first, is_second)
    ]
    return ((first, ranks[0]), (second, ranks[1]))


def wide_row(expert, rank):
    return jnp.where(rank < 8, expert * 8 + rank, -1)


def half_row(expert, rank, half):
    return jnp.where(rank >= 8, expert * 8 + half * 4 + rank - 8, -1)


def as_column(row):
    toks = row.shape[1]
    eye = iota((toks, toks), 0) == iota((toks, toks), 1)
    return jnp.sum(jnp.where(eye, row, jnp.zeros_like(row)), axis=1, keepdims=True)


def send_masks(experts_ref, count):
    rows = count * 8
    toks = experts_ref.shape[1]
    row = iota((rows, toks), 0)
    out = []
    for expert, rank in pick_ranks(experts_ref, count):
        out.append(
            (
                row == wide_row(expert, rank),
                row == half_row(expert, rank, 0),
                row == half_row(expert, rank, 1),
            )
        )
    return out


def one_hot(*masks):
    both = masks[0]
    for mask in masks[1:]:
        both = both | mask
    return jnp.where(both, 1.0, 0.0).astype(BF)


def pack_tokens(experts_ref, rows_ref, out_ref, rows_in, sems):
    count = out_ref.shape[0] // 8
    width = rows_ref.shape[1]
    half = width // 2
    copies = [
        pltpu.make_async_copy(
            rows_ref.at[:, pl.ds(i * half, half)], rows_in.at[:, pl.ds(i * half, half)], sems.at[i]
        )
        for i in range(2)
    ]
    for copy in copies:
        copy.start()
    first, second = send_masks(experts_ref, count)
    wide = one_hot(first[0], second[0])
    halves = [one_hot(first[1 + h], second[1 + h]) for h in range(2)]
    for i in range(2):
        copies[i].wait()
        for c in range(i * half, (i + 1) * half, TILE):
            out_ref[:, c : c + TILE] = dot(wide, rows_in[:, c : c + TILE]).astype(BF)
    for c in range(0, half, TILE):
        out_ref[:, width + c : width + c + TILE] = (
            dot(halves[0], rows_in[:, c : c + TILE])
            + dot(halves[1], rows_in[:, half + c : half + c + TILE])
        ).astype(BF)


def pack_grads(experts_ref, gates_ref, rows_ref, out_ref):
    count = out_ref.shape[0] // 8
    width = rows_ref.shape[1]
    half = width // 2
    first, second = send_masks(experts_ref, count)
    gate0, gate1 = gates_ref[0:1, :], gates_ref[1:2, :]

    def gate_of(mask0, mask1):
        return jnp.sum(
            jnp.where(mask0, gate0, 0.0) + jnp.where(mask1, gate1, 0.0), axis=1, keepdims=True
        )

    wide = one_hot(first[0], second[0])
    wide_gate = gate_of(first[0], second[0])
    halves = [one_hot(first[1 + h], second[1 + h]) for h in range(2)]
    half_gate = gate_of(first[1] | first[2], second[1] | second[2])
    for c in range(0, width, TILE):
        out_ref[:, c : c + TILE] = (wide_gate * dot(wide, rows_ref[:, c : c + TILE])).astype(BF)
    for c in range(0, half, TILE):
        out_ref[:, width + c : width + c + TILE] = (
            half_gate
            * (
                dot(halves[0], rows_ref[:, c : c + TILE])
                + dot(halves[1], rows_ref[:, half + c : half + c + TILE])
            )
        ).astype(BF)


def fetch_masks(experts_ref, count):
    rows = count * 8
    toks = experts_ref.shape[1]
    col = iota((toks, rows), 1)
    out = []
    for expert, rank in pick_ranks(experts_ref, count):
        targets = (wide_row(expert, rank), half_row(expert, rank, 0), half_row(expert, rank, 1))
        out.append(tuple(col == as_column(t) for t in targets))
    return out


def combine_out(experts_ref, gates_ref, got_ref, grad_ref, mixed_ref, gate_grad_ref):
    count = got_ref.shape[0] // 8
    toks, width = mixed_ref.shape
    half = width // 2
    masks = fetch_masks(experts_ref, count)
    wide = [one_hot(m[0]) for m in masks]
    halves = [[one_hot(m[1 + h]) for m in masks] for h in range(2)]
    gates = [as_column(gates_ref[k : k + 1, :]) for k in range(2)]
    sums = [jnp.zeros((toks, 1), F32) for _ in range(2)]
    for c in range(0, width, TILE):
        h, low = c // half, width + c % half
        grad = grad_ref[:, c : c + TILE].astype(F32)
        total = jnp.zeros((toks, TILE), F32)
        for k in range(2):
            picked = dot(wide[k], got_ref[:, c : c + TILE]) + dot(
                halves[h][k], got_ref[:, low : low + TILE]
            )
            total = total + gates[k] * picked
            sums[k] = sums[k] + jnp.sum(grad * picked, axis=1, keepdims=True)
        mixed_ref[:, c : c + TILE] = total.astype(BF)
    lane = iota((toks, 2), 1)
    gate_grad_ref[...] = jnp.where(lane == 0, sums[0], sums[1])


def combine_grads(experts_ref, got_ref, out_ref, got_in, sems):
    count = got_ref.shape[0] // 8
    width = out_ref.shape[1]
    half = width // 2
    pieces = ((width, half), (0, half), (half, half))
    copies = [
        pltpu.make_async_copy(
            got_ref.at[:, pl.ds(at, size)], got_in.at[:, pl.ds(at, size)], sems.at[i]
        )
        for i, (at, size) in enumerate(pieces)
    ]
    for copy in copies:
        copy.start()
    first, second = fetch_masks(experts_ref, count)
    wide = one_hot(first[0], second[0])
    halves = [one_hot(first[1 + h], second[1 + h]) for h in range(2)]
    copies[0].wait()
    for h in range(2):
        copies[1 + h].wait()
        for c in range(0, half, TILE):
            at = h * half + c
            out_ref[:, at : at + TILE] = (
                dot(wide, got_in[:, at : at + TILE])
                + dot(halves[h], got_in[:, width + c : width + c + TILE])
            ).astype(BF)


def split_rows(got_ref, rows_ref):
    count = got_ref.shape[0]
    width = rows_ref.shape[1]
    half = width // 2
    tail = count // 2
    rows_ref[0:count, :] = got_ref[:, 0:width]
    row, col = iota((tail, count), 0), iota((tail, count), 1)
    for h in range(2):
        pick = one_hot(col == (row >> 2) * 8 + h * 4 + (row & 3))
        for c in range(0, half, TILE):
            rows_ref[count : count + tail, h * half + c : h * half + c + TILE] = dot(
                pick, got_ref[:, width + c : width + c + TILE]
            ).astype(BF)


def tail_spread(count):
    tail = count // 2
    row, col = iota((count, tail), 0), iota((count, tail), 1)
    return [one_hot(row == (col >> 2) * 8 + h * 4 + (col & 3)) for h in range(2)]


def store_rows(product, send_ref, tail_ref, width, at, size):
    count = send_ref.shape[0]
    send_ref[:, at : at + size] = product[0:count]
    tail_ref[:, at : at + size] = product[count:]


def flush_tail(send_ref, tail_ref, width):
    count = send_ref.shape[0]
    half = width // 2
    spread = tail_spread(count)
    for c in range(0, half, TILE):
        send_ref[:, width + c : width + c + TILE] = (
            dot(spread[0], tail_ref[:, c : c + TILE])
            + dot(spread[1], tail_ref[:, half + c : half + c + TILE])
        ).astype(BF)


def forward_rows(
    block, core_ref, got_ref, weights_ref, send_ref, turned_ref, gate_ref, up_ref, rows_ref, hidden_ref, tail_ref
):
    width = rows_ref.shape[1]
    hid = gate_ref.shape[1]
    split_rows(got_ref, rows_ref)
    for c in range(0, hid, 256):
        gate = dot(rows_ref[...], weights_ref[:, c : c + 256])
        up = dot(rows_ref[...], weights_ref[:, hid + c : hid + c + 256])
        gate_ref[:, c : c + 256] = gate
        up_ref[:, c : c + 256] = up
        hidden_ref[:, c : c + 256] = (gate * jax.nn.sigmoid(gate) * up).astype(BF)
    for c in range(0, width, 256):
        product = dot_cols(hidden_ref[...], weights_ref[c : c + 256, 2 * hid : 3 * hid]).astype(BF)
        store_rows(product, send_ref, tail_ref, width, c, 256)
    flush_tail(send_ref, tail_ref, width)
    core = core_ref[0]
    for side, owner in enumerate((core, 1 - core)):
        for c in range(0, width // 2, block):
            at = pl.multiple_of(2 * c + owner * block, 128)
            to = side * (width // 2) + c
            turned_ref[:, to : to + block] = rows_ref[:, pl.ds(at, block)]


def backward_hidden(
    got_ref, weights_ref, gate_ref, up_ref, turned_ref,
    pre_ref, keep_ref, give_ref,
    rows_ref, down_in, gate_in, up_in, turned_in, sums_ref, sems, out_sems,
):
    width = rows_ref.shape[1]
    hid = gate_ref.shape[1]
    copies = [
        pltpu.make_async_copy(source, target, sems.at[i])
        for i, (source, target) in enumerate(
            (
                (weights_ref.at[:, pl.ds(2 * hid, hid)], down_in),
                (gate_ref, gate_in),
                (up_ref, up_in),
                (turned_ref, turned_in),
            )
        )
    ]
    for copy in copies:
        copy.start()
    split_rows(got_ref, rows_ref)
    for copy in copies[:3]:
        copy.wait()
    for c in range(0, hid, 256):
        grad = dot(rows_ref[...], down_in[:, c : c + 256])
        gate, up = gate_in[:, c : c + 256], up_in[:, c : c + 256]
        sigma = jax.nn.sigmoid(gate)
        pre_ref[:, hid + c : hid + c + 256] = (grad * gate * sigma).astype(BF)
        pre_ref[:, c : c + 256] = (grad * up * sigma * (1.0 + gate * (1.0 - sigma))).astype(BF)
    copies[3].wait()
    leaving = []
    for side, out_ref in ((1, give_ref), (0, keep_ref)):
        for c in range(0, width // 2, 256):
            at = side * (width // 2) + c
            sums_ref[at : at + 256, :] = lax.dot_general(
                turned_in[:, at : at + 256],
                pre_ref[...],
                (((0,), (0,)), ((), ())),
                preferred_element_type=F32,
            ).astype(BF)
            leaving.append(
                pltpu.make_async_copy(
                    sums_ref.at[pl.ds(at, 256)], out_ref.at[pl.ds(c, 256)], out_sems.at[at // 256]
                )
            )
            leaving[-1].start()
    for copy in leaving:
        copy.wait()


def backward_rows(pre_ref, weights_ref, send_ref, both_in, tail_ref, sems):
    width = weights_ref.shape[0]
    both = pre_ref.shape[1]
    parts = 4
    size = width // parts
    copies = [
        pltpu.make_async_copy(
            weights_ref.at[pl.ds(i * size, size), pl.ds(0, both)],
            both_in.at[pl.ds(i * size, size)],
            sems.at[i],
        )
        for i in range(parts)
    ]
    for copy in copies:
        copy.start()
    for i in range(parts):
        copies[i].wait()
        for c in range(i * size, (i + 1) * size, 256):
            product = dot_cols(pre_ref[...], both_in[c : c + 256, :]).astype(BF)
            store_rows(product, send_ref, tail_ref, width, c, 256)
    flush_tail(send_ref, tail_ref, width)


def call(body, outs, scratch, flops, *args, far=(), far_outs=(), scalars=()):
    size = sum(a.size * a.dtype.itemsize for a in args)
    size += sum(o[0][0] * o[0][1] * jnp.dtype(o[1]).itemsize for o in outs)
    spaces = [
        pltpu.HBM if i in far else pltpu.SMEM if i in scalars else pltpu.VMEM for i in range(len(args))
    ]
    held = [pltpu.VMEM(*s) for s in scratch]
    if far:
        held.append(pltpu.SemaphoreType.DMA((4,)))
    if far_outs:
        held.append(pltpu.SemaphoreType.DMA((8,)))
    return pl.pallas_call(
        body,
        out_shape=[jax.ShapeDtypeStruct(s, d) for s, d in outs],
        in_specs=[pl.BlockSpec(memory_space=space) for space in spaces],
        out_specs=[
            pl.BlockSpec(memory_space=pltpu.HBM if i in far_outs else pltpu.VMEM)
            for i in range(len(outs))
        ],
        scratch_shapes=held,
        cost_estimate=pl.CostEstimate(flops=flops, bytes_accessed=size, transcendentals=0),
        compiler_params=pltpu.CompilerParams(vmem_limit_bytes=(58 if far else 12) << 20),
    )(*args)


def on_device(tokens, gates, experts, gate_weight, up_weight, down_weight, out_grad):
    toks, width = tokens.shape
    hid = gate_weight.shape[2]
    count = lax.axis_size("expert") * gate_weight.shape[0]
    send = (count * 8, 3 * width // 2)
    slots = count * 12
    experts_t, gates_t = experts.T, gates.T

    def exchange(rows):
        moved = lax.all_to_all(
            rows.reshape(count, 8, send[1]),
            "expert",
            split_axis=0,
            concat_axis=0,
            tiled=True,
            axis_index_groups=[[y * 4 + x for x in range(4) for y in range(8)]],
        )
        return moved.reshape(send)

    pack_flops = 2 * send[0] * toks * send[1]
    (send_tok,) = call(
        pack_tokens, [(send, BF)], [((toks, width), BF)], pack_flops, experts_t, tokens, far=(1,)
    )
    shards, send_tok = lax.optimization_barrier(((gate_weight, up_weight, down_weight), send_tok))
    weights = lax.all_gather(jnp.concatenate(shards, axis=2), "dp", axis=1, tiled=True)[0]
    (send_grad,) = call(pack_grads, [(send, BF)], [], pack_flops, experts_t, gates_t, out_grad)
    got_tok = exchange(send_tok)
    got_tok, send_grad = lax.optimization_barrier((got_tok, send_grad))
    got_grad = exchange(send_grad)
    core = (lax.axis_index("dp") % 2).astype(jnp.int32)[None]
    send_out, turned, gate_pre, up_pre = call(
        functools.partial(forward_rows, width // lax.axis_size("dp")),
        [(send, BF), ((slots, width), BF), ((slots, hid), F32), ((slots, hid), F32)],
        [((slots, width), BF), ((slots, hid), BF), ((slots - send[0], width), BF)],
        6 * slots * width * hid,
        core,
        got_tok,
        weights,
        scalars=(0,),
    )
    got_grad, send_out = lax.optimization_barrier((got_grad, send_out))
    got_out = exchange(send_out)
    half = (width // 2, 2 * hid)
    pre_grads, keep, give = call(
        backward_hidden,
        [((slots, 2 * hid), BF), (half, BF), (half, BF)],
        [
            ((slots, width), BF),
            ((width, hid), BF),
            ((slots, hid), F32),
            ((slots, hid), F32),
            ((slots, width), BF),
            ((width, 2 * hid), BF),
        ],
        6 * slots * width * hid,
        got_grad,
        weights,
        gate_pre,
        up_pre,
        turned,
        far=(1, 2, 3, 4),
        far_outs=(1, 2),
    )
    dp = lax.axis_size("dp")
    taken = lax.ppermute(give, "dp", [(i, i ^ 1) for i in range(dp)])
    pair = (keep.astype(F32) + taken.astype(F32)).astype(BF)
    summed = lax.psum_scatter(
        pair,
        "dp",
        scatter_dimension=0,
        tiled=True,
        axis_index_groups=[[i + c for i in range(0, dp, 2)] for c in range(2)],
    ).astype(F32)[None]
    (send_back,) = call(
        backward_rows,
        [(send, BF)],
        [((width, 2 * hid), BF), ((slots - send[0], width), BF)],
        4 * slots * width * hid,
        pre_grads,
        weights,
        far=(1,),
    )
    got_out, send_back = lax.optimization_barrier((got_out, send_back))
    got_back = exchange(send_back)
    mixed, gate_grad = call(
        combine_out,
        [((toks, width), BF), ((toks, 2), F32)],
        [],
        40000000 * toks * send[0] * width * 2,
        experts_t,
        gates_t,
        got_out,
        out_grad,
    )
    experts_t, summed = lax.optimization_barrier(
        (experts_t, (summed[:, :, :hid], summed[:, :, hid:]))
    )
    (token_grad,) = call(
        combine_grads,
        [((toks, width), BF)],
        [(send, BF)],
        4 * toks * send[0] * width,
        experts_t,
        got_back,
        far=(1,),
    )
    return (mixed, token_grad, gate_grad, *summed)


def solution(mesh):
    return jax.shard_map(
        on_device,
        mesh=mesh,
        in_specs=(
            P(("dp", "expert"), None),
            P(("dp", "expert"), None),
            P(("dp", "expert"), None),
            P("expert", "dp", None),
            P("expert", "dp", None),
            P("expert", "dp", None),
            P(("dp", "expert"), None),
        ),
        out_specs=(
            P(("dp", "expert"), None),
            P(("dp", "expert"), None),
            P(("dp", "expert"), None),
            P("expert", "dp", None),
            P("expert", "dp", None),
        ),
        check_vma=False,
    )
```

```python
import functools

import jax
import jax.numpy as jnp
from jax import lax
from jax.experimental import pallas as pl
from jax.experimental.pallas import tpu as pltpu
from jax.sharding import PartitionSpec as P

BF = jnp.bfloat16
F32 = jnp.float32
TILE = 512


def iota(shape, axis):
    return lax.broadcasted_iota(jnp.int32, shape, axis)


def dot(left, right):
    return jnp.dot(left, right, preferred_element_type=F32)


def dot_cols(left, right):
    return lax.dot_general(left, right, (((1,), (1,)), ((), ())), preferred_element_type=F32)


NEAR_FIRST = (0, 1, 7, 2, 6, 3, 5, 4)


def turn(expert):
    y = expert >> 2
    return (expert & 3) * 8 + jnp.where(y > 4, 16 - 2 * y, jnp.maximum(2 * y - 1, 0))


def pick_ranks(experts_ref, count):
    first, second = turn(experts_ref[0:1, :]), turn(experts_ref[1:2, :])
    toks = experts_ref.shape[1]
    names = iota((count, toks), 0)
    is_first, is_second = names == first, names == second
    either = jnp.where(is_first | is_second, 1.0, 0.0).astype(BF)
    earlier = jnp.where(iota((toks, toks), 0) < iota((toks, toks), 1), 1.0, 0.0).astype(BF)
    before = dot(either, earlier)
    ranks = [
        jnp.sum(jnp.where(mask, before, 0.0), axis=0, keepdims=True).astype(jnp.int32)
        for mask in (is_first, is_second)
    ]
    return ((first, ranks[0]), (second, ranks[1]))


def wide_row(expert, rank):
    return jnp.where(rank < 8, expert * 8 + rank, -1)


def half_row(expert, rank, half):
    return jnp.where(rank >= 8, expert * 8 + half * 4 + rank - 8, -1)


def as_column(row):
    toks = row.shape[1]
    eye = iota((toks, toks), 0) == iota((toks, toks), 1)
    return jnp.sum(jnp.where(eye, row, jnp.zeros_like(row)), axis=1, keepdims=True)


def send_masks(experts_ref, count):
    rows = count * 8
    toks = experts_ref.shape[1]
    row = iota((rows, toks), 0)
    out = []
    for expert, rank in pick_ranks(experts_ref, count):
        out.append(
            (
                row == wide_row(expert, rank),
                row == half_row(expert, rank, 0),
                row == half_row(expert, rank, 1),
            )
        )
    return out


def one_hot(*masks):
    both = masks[0]
    for mask in masks[1:]:
        both = both | mask
    return jnp.where(both, 1.0, 0.0).astype(BF)


def pack_tokens(experts_ref, rows_ref, out_ref):
    count = out_ref.shape[0] // 8
    width = rows_ref.shape[1]
    half = width // 2
    first, second = send_masks(experts_ref, count)
    wide = one_hot(first[0], second[0])
    halves = [one_hot(first[1 + h], second[1 + h]) for h in range(2)]
    for c in range(0, width, TILE):
        out_ref[:, c : c + TILE] = dot(wide, rows_ref[:, c : c + TILE]).astype(BF)
    for c in range(0, half, TILE):
        out_ref[:, width + c : width + c + TILE] = (
            dot(halves[0], rows_ref[:, c : c + TILE])
            + dot(halves[1], rows_ref[:, half + c : half + c + TILE])
        ).astype(BF)


def pack_grads(experts_ref, gates_ref, rows_ref, out_ref):
    count = out_ref.shape[0] // 8
    width = rows_ref.shape[1]
    half = width // 2
    first, second = send_masks(experts_ref, count)
    gate0, gate1 = gates_ref[0:1, :], gates_ref[1:2, :]

    def gate_of(mask0, mask1):
        return jnp.sum(
            jnp.where(mask0, gate0, 0.0) + jnp.where(mask1, gate1, 0.0), axis=1, keepdims=True
        )

    wide = one_hot(first[0], second[0])
    wide_gate = gate_of(first[0], second[0])
    halves = [one_hot(first[1 + h], second[1 + h]) for h in range(2)]
    half_gate = gate_of(first[1] | first[2], second[1] | second[2])
    for c in range(0, width, TILE):
        out_ref[:, c : c + TILE] = (wide_gate * dot(wide, rows_ref[:, c : c + TILE])).astype(BF)
    for c in range(0, half, TILE):
        out_ref[:, width + c : width + c + TILE] = (
            half_gate
            * (
                dot(halves[0], rows_ref[:, c : c + TILE])
                + dot(halves[1], rows_ref[:, half + c : half + c + TILE])
            )
        ).astype(BF)


def fetch_masks(experts_ref, count):
    rows = count * 8
    toks = experts_ref.shape[1]
    col = iota((toks, rows), 1)
    out = []
    for expert, rank in pick_ranks(experts_ref, count):
        targets = (wide_row(expert, rank), half_row(expert, rank, 0), half_row(expert, rank, 1))
        out.append(tuple(col == as_column(t) for t in targets))
    return out


def combine_out(experts_ref, gates_ref, got_ref, grad_ref, mixed_ref, gate_grad_ref):
    count = got_ref.shape[0] // 8
    toks, width = mixed_ref.shape
    half = width // 2
    masks = fetch_masks(experts_ref, count)
    wide = [one_hot(m[0]) for m in masks]
    halves = [[one_hot(m[1 + h]) for m in masks] for h in range(2)]
    gates = [as_column(gates_ref[k : k + 1, :]) for k in range(2)]
    sums = [jnp.zeros((toks, 1), F32) for _ in range(2)]
    for c in range(0, width, TILE):
        h, low = c // half, width + c % half
        grad = grad_ref[:, c : c + TILE].astype(F32)
        total = jnp.zeros((toks, TILE), F32)
        for k in range(2):
            picked = dot(wide[k], got_ref[:, c : c + TILE]) + dot(
                halves[h][k], got_ref[:, low : low + TILE]
            )
            total = total + gates[k] * picked
            sums[k] = sums[k] + jnp.sum(grad * picked, axis=1, keepdims=True)
        mixed_ref[:, c : c + TILE] = total.astype(BF)
    lane = iota((toks, 2), 1)
    gate_grad_ref[...] = jnp.where(lane == 0, sums[0], sums[1])


def combine_grads(experts_ref, got_ref, out_ref):
    count = got_ref.shape[0] // 8
    width = out_ref.shape[1]
    half = width // 2
    first, second = fetch_masks(experts_ref, count)
    wide = one_hot(first[0], second[0])
    halves = [one_hot(first[1 + h], second[1 + h]) for h in range(2)]
    for c in range(0, width, TILE):
        low = width + c % half
        out_ref[:, c : c + TILE] = (
            dot(wide, got_ref[:, c : c + TILE]) + dot(halves[c // half], got_ref[:, low : low + TILE])
        ).astype(BF)


def split_rows(got_ref, rows_ref):
    count = got_ref.shape[0]
    width = rows_ref.shape[1]
    half = width // 2
    tail = count // 2
    rows_ref[0:count, :] = got_ref[:, 0:width]
    row, col = iota((tail, count), 0), iota((tail, count), 1)
    for h in range(2):
        pick = one_hot(col == (row >> 2) * 8 + h * 4 + (row & 3))
        for c in range(0, half, TILE):
            rows_ref[count : count + tail, h * half + c : h * half + c + TILE] = dot(
                pick, got_ref[:, width + c : width + c + TILE]
            ).astype(BF)


def tail_spread(count):
    tail = count // 2
    row, col = iota((count, tail), 0), iota((count, tail), 1)
    return [one_hot(row == (col >> 2) * 8 + h * 4 + (col & 3)) for h in range(2)]


def store_rows(product, send_ref, tail_ref, width, at, size):
    count = send_ref.shape[0]
    send_ref[:, at : at + size] = product[0:count]
    tail_ref[:, at : at + size] = product[count:]


def flush_tail(send_ref, tail_ref, width):
    count = send_ref.shape[0]
    half = width // 2
    spread = tail_spread(count)
    for c in range(0, half, TILE):
        send_ref[:, width + c : width + c + TILE] = (
            dot(spread[0], tail_ref[:, c : c + TILE])
            + dot(spread[1], tail_ref[:, half + c : half + c + TILE])
        ).astype(BF)


def forward_rows(
    block, core_ref, got_ref, weights_ref, send_ref, turned_ref, gate_ref, up_ref, rows_ref, hidden_ref, tail_ref
):
    width = rows_ref.shape[1]
    hid = gate_ref.shape[1]
    split_rows(got_ref, rows_ref)
    for c in range(0, hid, 256):
        gate = dot(rows_ref[...], weights_ref[:, c : c + 256])
        up = dot(rows_ref[...], weights_ref[:, hid + c : hid + c + 256])
        gate_ref[:, c : c + 256] = gate
        up_ref[:, c : c + 256] = up
        hidden_ref[:, c : c + 256] = (gate * jax.nn.sigmoid(gate) * up).astype(BF)
    for c in range(0, width, 256):
        product = dot_cols(hidden_ref[...], weights_ref[c : c + 256, 2 * hid : 3 * hid]).astype(BF)
        store_rows(product, send_ref, tail_ref, width, c, 256)
    flush_tail(send_ref, tail_ref, width)
    core = core_ref[0]
    for side, owner in enumerate((core, 1 - core)):
        for c in range(0, width // 2, block):
            at = pl.multiple_of(2 * c + owner * block, 128)
            to = side * (width // 2) + c
            turned_ref[:, to : to + block] = rows_ref[:, pl.ds(at, block)]


def backward_hidden(
    got_ref, weights_ref, gate_ref, up_ref, turned_ref,
    pre_ref, keep_ref, give_ref,
    rows_ref, down_in, gate_in, up_in, turned_in, sums_ref, sems, out_sems,
):
    width = rows_ref.shape[1]
    hid = gate_ref.shape[1]
    copies = [
        pltpu.make_async_copy(source, target, sems.at[i])
        for i, (source, target) in enumerate(
            (
                (weights_ref.at[:, pl.ds(2 * hid, hid)], down_in),
                (gate_ref, gate_in),
                (up_ref, up_in),
                (turned_ref, turned_in),
            )
        )
    ]
    for copy in copies:
        copy.start()
    split_rows(got_ref, rows_ref)
    for copy in copies[:3]:
        copy.wait()
    for c in range(0, hid, 256):
        grad = dot(rows_ref[...], down_in[:, c : c + 256])
        gate, up = gate_in[:, c : c + 256], up_in[:, c : c + 256]
        sigma = jax.nn.sigmoid(gate)
        pre_ref[:, hid + c : hid + c + 256] = (grad * gate * sigma).astype(BF)
        pre_ref[:, c : c + 256] = (grad * up * sigma * (1.0 + gate * (1.0 - sigma))).astype(BF)
    copies[3].wait()
    leaving = []
    for side, out_ref in ((1, give_ref), (0, keep_ref)):
        for c in range(0, width // 2, 256):
            at = side * (width // 2) + c
            sums_ref[at : at + 256, :] = lax.dot_general(
                turned_in[:, at : at + 256],
                pre_ref[...],
                (((0,), (0,)), ((), ())),
                preferred_element_type=F32,
            ).astype(BF)
            leaving.append(
                pltpu.make_async_copy(
                    sums_ref.at[pl.ds(at, 256)], out_ref.at[pl.ds(c, 256)], out_sems.at[at // 256]
                )
            )
            leaving[-1].start()
    for copy in leaving:
        copy.wait()


def backward_rows(pre_ref, weights_ref, send_ref, both_in, tail_ref, sems):
    width = weights_ref.shape[0]
    both = pre_ref.shape[1]
    parts = 4
    size = width // parts
    copies = [
        pltpu.make_async_copy(
            weights_ref.at[pl.ds(i * size, size), pl.ds(0, both)],
            both_in.at[pl.ds(i * size, size)],
            sems.at[i],
        )
        for i in range(parts)
    ]
    for copy in copies:
        copy.start()
    for i in range(parts):
        copies[i].wait()
        for c in range(i * size, (i + 1) * size, 256):
            product = dot_cols(pre_ref[...], both_in[c : c + 256, :]).astype(BF)
            store_rows(product, send_ref, tail_ref, width, c, 256)
    flush_tail(send_ref, tail_ref, width)


def call(body, outs, scratch, flops, *args, far=(), far_outs=(), scalars=()):
    size = sum(a.size * a.dtype.itemsize for a in args)
    size += sum(o[0][0] * o[0][1] * jnp.dtype(o[1]).itemsize for o in outs)
    spaces = [
        pltpu.HBM if i in far else pltpu.SMEM if i in scalars else pltpu.VMEM for i in range(len(args))
    ]
    held = [pltpu.VMEM(*s) for s in scratch]
    if far:
        held.append(pltpu.SemaphoreType.DMA((4,)))
    if far_outs:
        held.append(pltpu.SemaphoreType.DMA((8,)))
    return pl.pallas_call(
        body,
        out_shape=[jax.ShapeDtypeStruct(s, d) for s, d in outs],
        in_specs=[pl.BlockSpec(memory_space=space) for space in spaces],
        out_specs=[
            pl.BlockSpec(memory_space=pltpu.HBM if i in far_outs else pltpu.VMEM)
            for i in range(len(outs))
        ],
        scratch_shapes=held,
        cost_estimate=pl.CostEstimate(flops=flops, bytes_accessed=size, transcendentals=0),
        compiler_params=pltpu.CompilerParams(vmem_limit_bytes=(58 if far else 12) << 20),
    )(*args)


def on_device(tokens, gates, experts, gate_weight, up_weight, down_weight, out_grad):
    toks, width = tokens.shape
    hid = gate_weight.shape[2]
    count = lax.axis_size("expert") * gate_weight.shape[0]
    send = (count * 8, 3 * width // 2)
    slots = count * 12
    experts_t, gates_t = experts.T, gates.T

    def exchange(rows):
        moved = lax.all_to_all(
            rows.reshape(count, 8, send[1]),
            "expert",
            split_axis=0,
            concat_axis=0,
            tiled=True,
            axis_index_groups=[[y * 4 + x for x in range(4) for y in NEAR_FIRST]],
        )
        return moved.reshape(send)

    pack_flops = 2 * send[0] * toks * send[1]
    (send_tok,) = call(pack_tokens, [(send, BF)], [], pack_flops, experts_t, tokens)
    shards, send_tok = lax.optimization_barrier(((gate_weight, up_weight, down_weight), send_tok))
    weights = lax.all_gather(jnp.concatenate(shards, axis=2), "dp", axis=1, tiled=True)[0]
    (send_grad,) = call(pack_grads, [(send, BF)], [], pack_flops, experts_t, gates_t, out_grad)
    got_tok = exchange(send_tok)
    got_tok, send_grad = lax.optimization_barrier((got_tok, send_grad))
    got_grad = exchange(send_grad)
    core = (lax.axis_index("dp") % 2).astype(jnp.int32)[None]
    send_out, turned, gate_pre, up_pre = call(
        functools.partial(forward_rows, width // lax.axis_size("dp")),
        [(send, BF), ((slots, width), BF), ((slots, hid), F32), ((slots, hid), F32)],
        [((slots, width), BF), ((slots, hid), BF), ((slots - send[0], width), BF)],
        6 * slots * width * hid,
        core,
        got_tok,
        weights,
        scalars=(0,),
    )
    got_grad, send_out = lax.optimization_barrier((got_grad, send_out))
    got_out = exchange(send_out)
    half = (width // 2, 2 * hid)
    pre_grads, keep, give = call(
        backward_hidden,
        [((slots, 2 * hid), BF), (half, BF), (half, BF)],
        [
            ((slots, width), BF),
            ((width, hid), BF),
            ((slots, hid), F32),
            ((slots, hid), F32),
            ((slots, width), BF),
            ((width, 2 * hid), BF),
        ],
        6 * slots * width * hid,
        got_grad,
        weights,
        gate_pre,
        up_pre,
        turned,
        far=(1, 2, 3, 4),
        far_outs=(1, 2),
    )
    dp = lax.axis_size("dp")
    taken = lax.ppermute(give, "dp", [(i, i ^ 1) for i in range(dp)])
    pair = (keep.astype(F32) + taken.astype(F32)).astype(BF)
    summed = lax.psum_scatter(
        pair,
        "dp",
        scatter_dimension=0,
        tiled=True,
        axis_index_groups=[[i + c for i in range(0, dp, 2)] for c in range(2)],
    ).astype(F32)[None]
    (send_back,) = call(
        backward_rows,
        [(send, BF)],
        [((width, 2 * hid), BF), ((slots - send[0], width), BF)],
        4 * slots * width * hid,
        pre_grads,
        weights,
        far=(1,),
    )
    got_out, send_back = lax.optimization_barrier((got_out, send_back))
    got_back = exchange(send_back)
    mixed, gate_grad = call(
        combine_out,
        [((toks, width), BF), ((toks, 2), F32)],
        [],
        40000000 * toks * send[0] * width * 2,
        experts_t,
        gates_t,
        got_out,
        out_grad,
    )
    experts_t, summed = lax.optimization_barrier(
        (experts_t, (summed[:, :, :hid], summed[:, :, hid:]))
    )
    (token_grad,) = call(
        combine_grads, [((toks, width), BF)], [], 4 * toks * send[0] * width, experts_t, got_back
    )
    return (mixed, token_grad, gate_grad, *summed)


def solution(mesh):
    return jax.shard_map(
        on_device,
        mesh=mesh,
        in_specs=(
            P(("dp", "expert"), None),
            P(("dp", "expert"), None),
            P(("dp", "expert"), None),
            P("expert", "dp", None),
            P("expert", "dp", None),
            P("expert", "dp", None),
            P(("dp", "expert"), None),
        ),
        out_specs=(
            P(("dp", "expert"), None),
            P(("dp", "expert"), None),
            P(("dp", "expert"), None),
            P("expert", "dp", None),
            P("expert", "dp", None),
        ),
        check_vma=False,
    )
```
